128 devices in a mesh: row: 8 (over y, z_hi), col: 8 (over z_lo, x), dp: 2 (over core).
Axes of the slice: x: 4, y: 4, z: 4 (z_hi: 2, z_lo: 2; z = z_hi * 2 + z_lo), core: 2. Of those that a mesh axis runs over, the one named last changes fastest.
Arguments:
- tokens: bfloat16 [2048, 4096], P(('col', 'dp'), 'row'), may hold values from -6 to 6
- grad_out: bfloat16 [2048, 4096], P(('col', 'dp'), 'row'), may hold values from -6 to 6
- gate_pre: bfloat16 [2048, 16384], P(('row', 'dp'), 'col'), may hold values from -8 to 8
- up_pre: bfloat16 [2048, 16384], P(('row', 'dp'), 'col'), may hold values from -6 to 6
- w_gate: bfloat16 [4096, 16384], P('row', 'col'), may hold values from -0.09375 to 0.09375
- w_up: bfloat16 [4096, 16384], P('row', 'col'), may hold values from -0.09375 to 0.09375
- w_down: bfloat16 [16384, 4096], P('col', 'row'), may hold values from -0.046875 to 0.046875
Outputs:
- grad_tokens: bfloat16 [2048, 4096], P(('col', 'dp'), 'row')
- grad_gate: bfloat16 [4096, 16384], P('row', 'col')
- grad_up: bfloat16 [4096, 16384], P('row', 'col')
- grad_down: bfloat16 [16384, 4096], P('col', 'row')
The draws below stay inside these ranges and needn't reach their ends.
All inputs are finite; a program needn't handle non-finite values.
Results may differ from the reference program's by a relative error of at most 0.0051.
Values may be sent and summed in bfloat16 or wider, within the bound.
No kernel may reach another device: no remote copies, remote signals or barrier semaphores. Data moves between devices by JAX's collectives and lax.ppermute only.
A program may use at most 128 MiB of HBM per device.

```python
import jax
import jax.numpy as jnp

D = 4096
FF = 16384
TOKENS = 2048


def levels(stream_key, dims, shards, least, largest):
    def one(position, shards_of):
        heights = jax.random.uniform(jax.random.fold_in(jax.random.fold_in(stream_key, 6), position), (shards_of,), jnp.float32, least / len(shards), largest / len(shards))
        return jnp.repeat(jnp.exp(heights), dims[position] // shards_of).reshape((-1,) + (1,) * (len(dims) - position - 1))

    factor_of = one(*shards[0])
    for cut in shards[1:]:
        factor_of = factor_of * one(*cut)
    return factor_of


def gaussian(key, dims, scale, bound, shards=(), held_as=jnp.bfloat16):
    loudness = levels(key, dims, shards, -0.22, 0.18) if shards else 1.0
    values = jax.random.normal(key, dims, jnp.float32) * scale * loudness
    return jnp.minimum(jnp.maximum(values, -bound), bound).astype(held_as)


def setup_inputs(seed: int = 0) -> dict:
    seeds = jax.random.split(jax.random.key(seed), 8)
    tokens = gaussian(seeds[0], (TOKENS, D), 1.0, 6.0, ((0, 16), (1, 8)))
    grad_out = gaussian(seeds[1], (TOKENS, D), 1.0, 6.0, ((0, 16), (1, 8)))
    gate_pre = gaussian(seeds[2], (TOKENS, FF), 1.5, 8.0, ((0, 16), (1, 8)))
    up_pre = gaussian(seeds[3], (TOKENS, FF), 1.0, 6.0, ((0, 16), (1, 8)))
    w_gate = gaussian(seeds[4], (D, FF), D ** -0.5, 0.09375, ((0, 8), (1, 8)))
    w_up = gaussian(seeds[5], (D, FF), D ** -0.5, 0.09375, ((0, 8), (1, 8)))
    w_down = gaussian(seeds[6], (FF, D), FF ** -0.5, 0.046875, ((0, 8), (1, 8)))
    return dict(tokens=tokens, grad_out=grad_out, gate_pre=gate_pre, up_pre=up_pre, w_gate=w_gate, w_up=w_up, w_down=w_down)


def reference(tokens, grad_out, gate_pre, up_pre, w_gate, w_up, w_down):
    gate_val = gate_pre.astype(jnp.float32)
    up_val = up_pre.astype(jnp.float32)
    sigmoid_gate = jax.nn.sigmoid(gate_val)
    active = gate_val * sigmoid_gate
    hidden = (active * up_val).astype(jnp.bfloat16)
    d_hidden = jnp.dot(grad_out, w_down.T, preferred_element_type=jnp.float32)
    d_gate = (d_hidden * up_val * sigmoid_gate * (1.0 + gate_val * (1.0 - sigmoid_gate))).astype(jnp.bfloat16)
    d_up = (d_hidden * active).astype(jnp.bfloat16)
    grad_tokens = (jnp.dot(d_gate, w_gate.T, preferred_element_type=jnp.float32) + jnp.dot(d_up, w_up.T, preferred_element_type=jnp.float32)).astype(jnp.bfloat16)
    factor = 1.0 / jnp.sqrt(jnp.float32(tokens.shape[0]))
    grad_gate = (jnp.dot(tokens.T, d_gate, preferred_element_type=jnp.float32) * factor).astype(jnp.bfloat16)
    grad_up = (jnp.dot(tokens.T, d_up, preferred_element_type=jnp.float32) * factor).astype(jnp.bfloat16)
    grad_down = (jnp.dot(hidden.T, grad_out, preferred_element_type=jnp.float32) * factor).astype(jnp.bfloat16)
    return (grad_tokens, grad_gate, grad_up, grad_down)
```

```python
import jax
import jax.numpy as jnp
from jax import lax
from jax.sharding import Mesh, PartitionSpec as P


COL = ("zl", "x")
BF = jnp.bfloat16
F32 = jnp.float32
SWAP = [(0, 1), (1, 0)]


def copies(x, n):
    return jnp.broadcast_to(x[None], (n,) + x.shape)


def gather_y(x):
    whole = lax.all_to_all(copies(x, 4), "y", 0, 0, tiled=True)
    return whole.reshape(4 * x.shape[0], x.shape[1])


def gather_col(x):
    return lax.all_to_all(copies(x, 8), COL, 0, 0, tiled=True)


def side(blocks, which):
    shaped = blocks.reshape(4, 2, blocks.shape[1], blocks.shape[2])
    picked = lax.dynamic_index_in_dim(shaped, which, 1, keepdims=False)
    return picked.reshape(4 * blocks.shape[1], blocks.shape[2])


def inner_rows(left, right):
    return lax.dot_general(left, right, (((0,), (0,)), ((), ())), preferred_element_type=F32)


def times_transposed(left, right):
    return lax.dot_general(left, right, (((1,), (1,)), ((), ())), preferred_element_type=F32)


def local(tokens, grad_out, gate_pre, up_pre, w_gate, w_up, w_down):
    rows, width = tokens.shape
    factor = 1.0 / jnp.sqrt(F32(16 * rows))
    zh = lax.axis_index("zh")

    out_blocks = gather_col(grad_out)
    out_own, out_oth = side(out_blocks, zh), side(out_blocks, 1 - zh)

    gate_own = gather_y(gate_pre)
    gate_oth = lax.ppermute(gate_own, "zh", SWAP)
    up_swap = lax.ppermute(up_pre, "zh", SWAP)
    up_own, up_oth = gather_y(up_pre), gather_y(up_swap)

    part_oth = times_transposed(out_oth, w_down).astype(BF)
    from_pair = lax.ppermute(part_oth, "zh", SWAP)
    part = (times_transposed(out_own, w_down) + from_pair.astype(F32)).astype(BF)
    pieces = lax.all_to_all(part.reshape(4, rows, -1), "y", 0, 0, tiled=True)
    d_mine = jnp.sum(pieces.astype(F32), axis=0).astype(BF)
    d_swap = lax.ppermute(d_mine, "zh", SWAP)
    d_own, d_oth = gather_y(d_mine), gather_y(d_swap)

    tok_blocks = gather_col(tokens)
    tok_own, tok_oth = side(tok_blocks, zh), side(tok_blocks, 1 - zh)

    def pointwise(gate, up, d):
        gate, up, d = gate.astype(F32), up.astype(F32), d.astype(F32)
        s = jax.nn.sigmoid(gate)
        active = gate * s
        hidden = (active * up).astype(BF)
        d_gate = (d * up * s * (1.0 + gate * (1.0 - s))).astype(BF)
        d_up = (d * active).astype(BF)
        return hidden, d_gate, d_up

    hid_own, dg_own, du_own = pointwise(gate_own, up_own, d_own)
    hid_oth, dg_oth, du_oth = pointwise(gate_oth, up_oth, d_oth)

    def back(dg, du):
        return (times_transposed(dg, w_gate) + times_transposed(du, w_up)).astype(BF)

    t_own = back(dg_own, du_own).reshape(4, rows, width)
    t_oth = back(dg_oth, du_oth).reshape(4, rows, width)
    first = jnp.where(zh == 0, t_own, t_oth)
    second = jnp.where(zh == 0, t_oth, t_own)
    t_parts = jnp.stack([first, second], axis=1).reshape(8, rows, width)
    t_recv = lax.all_to_all(t_parts, COL, 0, 0, tiled=True)
    grad_tokens = jnp.sum(t_recv.astype(F32), axis=0).astype(BF)

    def both_cores(total):
        mine = (total * factor).astype(BF)
        theirs = lax.ppermute(mine, "core", SWAP)
        return (mine.astype(F32) + theirs.astype(F32)).astype(BF)

    grad_down = both_cores(inner_rows(hid_own, out_own) + inner_rows(hid_oth, out_oth))
    grad_gate = both_cores(inner_rows(tok_own, dg_own) + inner_rows(tok_oth, dg_oth))
    grad_up = both_cores(inner_rows(tok_own, du_own) + inner_rows(tok_oth, du_oth))
    return grad_tokens, grad_gate, grad_up, grad_down


def solution(mesh):
    fine = Mesh(mesh.devices.reshape(4, 2, 2, 4, 2), ("y", "zh", "zl", "x", "core"))
    row, col = ("y", "zh"), COL
    act = P(col + ("core",), row)
    pre = P(row + ("core",), col)
    up = P(row, col)
    down = P(col, row)
    return jax.shard_map(
        local,
        mesh=fine,
        in_specs=(act, act, pre, pre, up, up, down),
        out_specs=(act, up, up, down),
        check_vma=False,
    )
```

```python
import functools

import jax
import jax.numpy as jnp
from jax import lax
from jax.experimental import pallas as pl
from jax.experimental.pallas import tpu as pltpu
from jax.sharding import Mesh, PartitionSpec as P


COL = ("zl", "x")
BF = jnp.bfloat16
F32 = jnp.float32
SWAP = [(0, 1), (1, 0)]
STEP = 256


def ring(shift):
    return [(i, (i + shift) % 4) for i in range(4)]


def along_y(x, shift):
    return lax.ppermute(x, "y", ring(shift))


def to_pair(x):
    return lax.ppermute(x, "zh", SWAP)


def gather_col(x):
    whole = lax.all_to_all(jnp.broadcast_to(x[None], (8,) + x.shape), COL, 0, 0, tiled=True)
    return whole.reshape(8 * x.shape[0], x.shape[1])


def inner_rows(left, right):
    return lax.dot_general(left, right, (((0,), (0,)), ((), ())), preferred_element_type=F32)


def times_transposed(left, right):
    return lax.dot_general(left, right, (((1,), (1,)), ((), ())), preferred_element_type=F32)


def place(where, p, rows):
    return pl.ds(pl.multiple_of(where[p] * rows, rows), rows)


def hidden_kernel(where, *refs):
    gates, ups, out = refs[:8], refs[8:16], refs[16]
    rows = gates[0].shape[0]
    for p in range(8):
        g = gates[p][...].astype(F32)
        u = ups[p][...].astype(F32)
        out[place(where, p, rows), :] = (g * jax.nn.sigmoid(g) * u).astype(BF)


def hidden_of(where, gates, ups):
    rows, width = gates[0].shape
    piece = pl.BlockSpec((rows, STEP), lambda c, w: (0, c))
    return pl.pallas_call(
        hidden_kernel,
        out_shape=jax.ShapeDtypeStruct((8 * rows, width), BF),
        grid_spec=pltpu.PrefetchScalarGridSpec(
            num_scalar_prefetch=1,
            grid=(width // STEP,),
            in_specs=[piece] * 16,
            out_specs=pl.BlockSpec((8 * rows, STEP), lambda c, w: (0, c)),
        ),
        cost_estimate=pl.CostEstimate(
            flops=8 * rows * width * 8, bytes_accessed=8 * rows * width * 6, transcendentals=8 * rows * width * 2
        ),
    )(where, *gates, *ups)


def back_kernel(where, *refs):
    gates, ups, ds = refs[:8], refs[8:16], refs[16:24]
    w_gate, w_up, d_gate, d_up, back, total = refs[24:]
    rows = gates[0].shape[0]
    c = pl.program_id(0)
    for p in range(8):
        g = gates[p][...].astype(F32)
        u = ups[p][...].astype(F32)
        d = ds[p][...].astype(F32)
        s = jax.nn.sigmoid(g)
        d_gate[place(where, p, rows), :] = (d * u * s * (1.0 + g * (1.0 - s))).astype(BF)
        d_up[place(where, p, rows), :] = (d * (g * s)).astype(BF)
    more = times_transposed(d_gate[...], w_gate[...]) + times_transposed(d_up[...], w_up[...])

    @pl.when(c == 0)
    def _():
        total[...] = more

    @pl.when(c > 0)
    def _():
        total[...] += more

    @pl.when(c == pl.num_programs(0) - 1)
    def _():
        back[...] = total[...].astype(BF)


def back_of(where, gates, ups, ds, w_gate, w_up):
    rows, width = gates[0].shape
    depth = w_gate.shape[0]
    piece = pl.BlockSpec((rows, STEP), lambda c, w: (0, c))
    weight = pl.BlockSpec((depth, STEP), lambda c, w: (0, c))
    full = pl.BlockSpec((8 * rows, STEP), lambda c, w: (0, c))
    return pl.pallas_call(
        back_kernel,
        out_shape=(
            jax.ShapeDtypeStruct((8 * rows, width), BF),
            jax.ShapeDtypeStruct((8 * rows, width), BF),
            jax.ShapeDtypeStruct((8 * rows, depth), BF),
        ),
        grid_spec=pltpu.PrefetchScalarGridSpec(
            num_scalar_prefetch=1,
            grid=(width // STEP,),
            in_specs=[piece] * 24 + [weight] * 2,
            out_specs=(full, full, pl.BlockSpec((8 * rows, depth), lambda c, w: (0, 0))),
            scratch_shapes=[pltpu.VMEM((8 * rows, depth), F32)],
        ),
        cost_estimate=pl.CostEstimate(
            flops=4 * 8 * rows * width * depth, bytes_accessed=8 * rows * width * 10, transcendentals=8 * rows * width * 2
        ),
    )(where, *gates, *ups, *ds, w_gate, w_up)


def local(tokens, grad_out, gate_pre, up_pre, w_gate, w_up, w_down):
    rows, width = tokens.shape
    factor = 1.0 / jnp.sqrt(F32(16 * rows))
    y, zh = lax.axis_index("y"), lax.axis_index("zh")
    where = jnp.stack([lax.rem(y + k, 4) * 2 + (zh if j == 0 else 1 - zh) for k in range(4) for j in range(2)])
    where = where.astype(jnp.int32)

    out_all = gather_col(grad_out)

    g3, g1 = along_y(gate_pre, 1), along_y(gate_pre, -1)
    u3, u1 = along_y(up_pre, 1), along_y(up_pre, -1)
    g2, u2 = along_y(g3, 1), along_y(u1, -1)
    gates = [v for g in (gate_pre, g1, g2, g3) for v in (g, to_pair(g))]
    ups = [v for u in (up_pre, u1, u2, u3) for v in (u, to_pair(u))]

    def part(k):
        here = lax.dynamic_slice_in_dim(out_all, lax.rem(y + k, 4) * (2 * rows), 2 * rows, 0)
        return times_transposed(here, w_down)

    recv = [along_y(part(k).astype(BF), k) for k in (2, 1, 3)]
    total = part(0) + sum(r.astype(F32) for r in recv)
    total = total.reshape(2, rows, -1)
    theirs = lax.dynamic_index_in_dim(total, 1 - zh, 0, keepdims=False).astype(BF)
    mine = lax.dynamic_index_in_dim(total, zh, 0, keepdims=False)
    d00 = (mine + to_pair(theirs).astype(F32)).astype(BF)
    d30, d10 = along_y(d00, 1), along_y(d00, -1)
    d01 = to_pair(d00)
    d31, d11 = along_y(d01, 1), along_y(d01, -1)
    d20, d21 = along_y(d30, 1), along_y(d11, -1)
    ds = [d00, d01, d10, d11, d20, d21, d30, d31]

    tok_all = gather_col(tokens)

    def both_cores(partial):
        own = (partial * factor).astype(BF)
        other = lax.ppermute(own, "core", SWAP)
        return (own.astype(F32) + other.astype(F32)).astype(BF)

    grad_down = both_cores(inner_rows(hidden_of(where, gates, ups), out_all))
    d_gate, d_up, back = back_of(where, gates, ups, ds, w_gate, w_up)
    back_recv = lax.all_to_all(back.reshape(8, rows, width), COL, 0, 0, tiled=True)
    grad_tokens = jnp.sum(back_recv.astype(F32), axis=0).astype(BF)
    grad_gate = both_cores(inner_rows(tok_all, d_gate))
    grad_up = both_cores(inner_rows(tok_all, d_up))
    return grad_tokens, grad_gate, grad_up, grad_down


def solution(mesh):
    fine = Mesh(mesh.devices.reshape(4, 2, 2, 4, 2), ("y", "zh", "zl", "x", "core"))
    row, col = ("y", "zh"), COL
    act = P(col + ("core",), row)
    pre = P(row + ("core",), col)
    up = P(row, col)
    down = P(col, row)
    return jax.shard_map(
        local,
        mesh=fine,
        in_specs=(act, act, pre, pre, up, up, down),
        out_specs=(act, up, up, down),
        check_vma=False,
    )
```

```python
import functools

import jax
import jax.numpy as jnp
import numpy as np
from jax import lax
from jax.experimental import pallas as pl
from jax.experimental.pallas import tpu as pltpu
from jax.sharding import Mesh, PartitionSpec as P


COL = ("zl", "x")
BF = jnp.bfloat16
F32 = jnp.float32
SWAP = [(0, 1), (1, 0)]
STEP = 256


def ring(shift):
    return [(i, (i + shift) % 4) for i in range(4)]


def along_y(x, shift):
    return lax.ppermute(x, "y", ring(shift))


def to_pair(x):
    return lax.ppermute(x, "zh", SWAP)


def across_col(x):
    return lax.all_to_all(x, COL, 0, 0, tiled=True)


def gather_col(x):
    many = jnp.broadcast_to(x[None], (8,) + x.shape)
    whole = across_col(many)
    return whole.reshape(8 * x.shape[0], x.shape[1])


def inner_rows(left, right):
    return lax.dot_general(left, right, (((0,), (0,)), ((), ())), preferred_element_type=F32)


def times_transposed(left, right):
    return lax.dot_general(left, right, (((1,), (1,)), ((), ())), preferred_element_type=F32)


def place(where, p, rows):
    return pl.ds(pl.multiple_of(where[p] * rows, rows), rows)


def hidden_kernel(where, *refs):
    gates, ups = refs[:8], refs[8:16]
    hidden, slope, active = refs[16:]
    rows = gates[0].shape[0]
    for p in range(8):
        g = gates[p][...].astype(F32)
        u = ups[p][...].astype(F32)
        s = jax.nn.sigmoid(g)
        here = place(where, p, rows)
        act = g * s
        hidden[here, :] = (act * u).astype(BF)
        slope[here, :] = u * s * (1.0 + g * (1.0 - s))
        active[here, :] = act


def hidden_of(where, gates, ups):
    rows, width = gates[0].shape
    total = 8 * rows
    piece = pl.BlockSpec((rows, STEP), lambda c, w: (0, c))
    full = pl.BlockSpec((total, STEP), lambda c, w: (0, c))
    return pl.pallas_call(
        hidden_kernel,
        out_shape=(
            jax.ShapeDtypeStruct((total, width), BF),
            jax.ShapeDtypeStruct((total, width), F32),
            jax.ShapeDtypeStruct((total, width), F32),
        ),
        grid_spec=pltpu.PrefetchScalarGridSpec(
            num_scalar_prefetch=1,
            grid=(width // STEP,),
            in_specs=[piece] * 16,
            out_specs=(full, full, full),
        ),
        cost_estimate=pl.CostEstimate(
            flops=total * width * 10, bytes_accessed=total * width * 14, transcendentals=total * width * 2
        ),
    )(where, *gates, *ups)


def back_kernel(factor, where, *refs):
    ds = refs[:8]
    slope, active, w_gate, w_up, tok, grad_gate, grad_up, back, d_gate, d_up, total = refs[8:]
    rows = ds[0].shape[0]
    c = pl.program_id(0)
    for p in range(8):
        d = ds[p][...].astype(F32)
        here = place(where, p, rows)
        d_gate[here, :] = (d * slope[here, :]).astype(BF)
        d_up[here, :] = (d * active[here, :]).astype(BF)
    dg, du = d_gate[...], d_up[...]
    more = times_transposed(dg, w_gate[...]) + times_transposed(du, w_up[...])
    grad_gate[...] = (jnp.dot(tok[...], dg, preferred_element_type=F32) * factor).astype(BF)
    grad_up[...] = (jnp.dot(tok[...], du, preferred_element_type=F32) * factor).astype(BF)

    @pl.when(c == 0)
    def _():
        total[...] = more

    @pl.when(c > 0)
    def _():
        total[...] += more

    @pl.when(c == pl.num_programs(0) - 1)
    def _():
        back[...] = total[...].astype(BF)


def back_of(where, ds, slope, active, w_gate, w_up, tok, factor):
    rows, width = ds[0].shape
    depth = w_gate.shape[0]
    total = 8 * rows
    piece = pl.BlockSpec((rows, STEP), lambda c, w: (0, c))
    weight = pl.BlockSpec((depth, STEP), lambda c, w: (0, c))
    full = pl.BlockSpec((total, STEP), lambda c, w: (0, c))
    return pl.pallas_call(
        functools.partial(back_kernel, factor),
        out_shape=(
            jax.ShapeDtypeStruct((depth, width), BF),
            jax.ShapeDtypeStruct((depth, width), BF),
            jax.ShapeDtypeStruct((total, depth), BF),
        ),
        grid_spec=pltpu.PrefetchScalarGridSpec(
            num_scalar_prefetch=1,
            grid=(width // STEP,),
            in_specs=[piece] * 8 + [full, full, weight, weight, pl.BlockSpec((depth, total), lambda c, w: (0, 0))],
            out_specs=(weight, weight, pl.BlockSpec((total, depth), lambda c, w: (0, 0))),
            scratch_shapes=[
                pltpu.VMEM((total, STEP), BF),
                pltpu.VMEM((total, STEP), BF),
                pltpu.VMEM((total, depth), F32),
            ],
        ),
        cost_estimate=pl.CostEstimate(
            flops=8 * total * width * depth, bytes_accessed=total * width * 14, transcendentals=0
        ),
    )(where, *ds, slope, active, w_gate, w_up, tok)


def local(tokens, grad_out, gate_pre, up_pre, w_gate, w_up, w_down):
    rows, width = tokens.shape
    factor = float(1.0 / np.sqrt(np.float32(16 * rows)))
    y, zh = lax.axis_index("y"), lax.axis_index("zh")
    p = lax.iota(jnp.int32, 8)
    where = lax.rem(y + p // 2, 4) * 2 + lax.rem(zh + p, 2)
    where_too = lax.rem(2 * y + (p & 6), 8) + (zh ^ (p & 1))

    out_all = gather_col(grad_out)

    g3, g1 = along_y(gate_pre, 1), along_y(gate_pre, -1)
    u3, u1 = along_y(up_pre, 1), along_y(up_pre, -1)
    g2, u2 = along_y(g3, 1), along_y(u1, -1)
    gates = [v for g in (gate_pre, g1, g2, g3) for v in (g, to_pair(g))]
    ups = [v for u in (up_pre, u1, u2, u3) for v in (u, to_pair(u))]

    def part(k):
        here = lax.dynamic_slice_in_dim(out_all, lax.rem(y + k, 4) * (2 * rows), 2 * rows, 0)
        return times_transposed(here, w_down).astype(BF if k else F32)

    recv = [along_y(part(k), k) for k in (2, 1, 3)]
    total = part(0) + sum(r.astype(F32) for r in recv)
    total = total.reshape(2, rows, -1)
    theirs = lax.dynamic_index_in_dim(total, 1 - zh, 0, keepdims=False).astype(BF)
    mine = lax.dynamic_index_in_dim(total, zh, 0, keepdims=False)
    d00 = (mine + to_pair(theirs).astype(F32)).astype(BF)
    d30, d10 = along_y(d00, 1), along_y(d00, -1)
    d01 = to_pair(d00)
    d31, d11 = along_y(d01, 1), along_y(d01, -1)
    d20, d21 = along_y(d30, 1), along_y(d11, -1)
    ds = [d00, d01, d10, d11, d20, d21, d30, d31]

    tok_all = gather_col(tokens)

    def both_cores(own):
        other = lax.ppermute(own, "core", SWAP)
        return (own.astype(F32) + other.astype(F32)).astype(BF)

    hidden, slope, active = hidden_of(where, gates, ups)
    down = (inner_rows(hidden, out_all) * factor).astype(BF)
    grad_down = both_cores(down)
    gate, up, back = back_of(where_too, ds, slope, active, w_gate, w_up, tok_all.T, factor)
    back_recv = across_col(back.reshape(8, rows, width))
    grad_gate = both_cores(gate)
    grad_up = both_cores(up)
    grad_tokens = jnp.sum(back_recv.astype(F32), axis=0).astype(BF)
    return grad_tokens, grad_gate, grad_up, grad_down


def solution(mesh):
    fine = Mesh(mesh.devices.reshape(4, 2, 2, 4, 2), ("y", "zh", "zl", "x", "core"))
    row, col = ("y", "zh"), COL
    act = P(col + ("core",), row)
    pre = P(row + ("core",), col)
    up = P(row, col)
    down = P(col, row)

    return jax.shard_map(
        local,
        mesh=fine,
        in_specs=(act, act, pre, pre, up, up, down),
        out_specs=(act, up, up, down),
        check_vma=False,
    )
```

```python
import functools

import jax
import jax.numpy as jnp
import numpy as np
from jax import lax
from jax.experimental import pallas as pl
from jax.experimental.pallas import tpu as pltpu
from jax.sharding import Mesh, PartitionSpec as P


COL = ("zl", "x")
BF = jnp.bfloat16
F32 = jnp.float32
SWAP = [(0, 1), (1, 0)]
STEP = 512


def ring(shift):
    return [(i, (i + shift) % 4) for i in range(4)]


def along_y(x, shift):
    return lax.ppermute(x, "y", ring(shift))


def to_pair(x):
    return lax.ppermute(x, "zh", SWAP)


def across_col(x):
    return lax.all_to_all(x, COL, 0, 0, tiled=True)


def gather_col(x):
    many = jnp.broadcast_to(x[None], (8,) + x.shape)
    whole = across_col(many)
    return whole.reshape(8 * x.shape[0], x.shape[1])


def inner_rows(left, right):
    return lax.dot_general(left, right, (((0,), (0,)), ((), ())), preferred_element_type=F32)


def times_transposed(left, right):
    return lax.dot_general(left, right, (((1,), (1,)), ((), ())), preferred_element_type=F32)


def place(where, p, rows):
    return pl.ds(pl.multiple_of(where[p] * rows, rows), rows)


def hidden_kernel(at, *refs):
    gates, ups = refs[:2], refs[2:4]
    hidden, slope, active = refs[-3:]
    rows = gates[0].shape[0]
    for j in range(2):
        g = gates[j][...].astype(F32)
        u = ups[j][...].astype(F32)
        s = jax.nn.sigmoid(g)
        here = place(at, 1 + j, rows)
        act = g * s
        hidden[here, :] = (act * u).astype(BF)
        slope[here, :] = u * s * (1.0 + g * (1.0 - s))
        active[here, :] = act


def hidden_of(at, gates, ups, before):
    rows, width = gates[0].shape
    total = 8 * rows
    piece = pl.BlockSpec((rows, STEP), lambda c, w: (0, c))
    pair = pl.BlockSpec((2 * rows, STEP), lambda c, w: (w[0], c))
    kept = [pl.BlockSpec(memory_space=pl.ANY)] * len(before)
    return pl.pallas_call(
        hidden_kernel,
        out_shape=(
            jax.ShapeDtypeStruct((total, width), BF),
            jax.ShapeDtypeStruct((total, width), F32),
            jax.ShapeDtypeStruct((total, width), F32),
        ),
        grid_spec=pltpu.PrefetchScalarGridSpec(
            num_scalar_prefetch=1,
            grid=(width // STEP,),
            in_specs=[piece] * 4 + kept,
            out_specs=(pair, pair, pair),
        ),
        input_output_aliases={5 + i: i for i in range(len(before))},
        cost_estimate=pl.CostEstimate(
            flops=2 * rows * width * 10, bytes_accessed=2 * rows * width * 14, transcendentals=2 * rows * width * 2
        ),
    )(at, *gates, *ups, *before)


def back_kernel(factor, where, *refs):
    ds = refs[:8]
    slope, active, w_gate, w_up, tok, grad_gate, grad_up, back, d_gate, d_up, total = refs[8:]
    rows = ds[0].shape[0]
    c = pl.program_id(0)
    for p in range(8):
        d = ds[p][...].astype(F32)
        here = place(where, p, rows)
        d_gate[here, :] = (d * slope[here, :]).astype(BF)
        d_up[here, :] = (d * active[here, :]).astype(BF)
    dg, du = d_gate[...], d_up[...]
    more = times_transposed(dg, w_gate[...]) + times_transposed(du, w_up[...])
    grad_gate[...] = (jnp.dot(tok[...], dg, preferred_element_type=F32) * factor).astype(BF)
    grad_up[...] = (jnp.dot(tok[...], du, preferred_element_type=F32) * factor).astype(BF)

    @pl.when(c == 0)
    def _():
        total[...] = more

    @pl.when(c > 0)
    def _():
        total[...] += more

    @pl.when(c == pl.num_programs(0) - 1)
    def _():
        back[...] = total[...].astype(BF)


def back_of(where, ds, slope, active, w_gate, w_up, tok, factor):
    rows, width = ds[0].shape
    depth = w_gate.shape[0]
    total = 8 * rows
    piece = pl.BlockSpec((rows, STEP), lambda c, w: (0, c))
    weight = pl.BlockSpec((depth, STEP), lambda c, w: (0, c))
    full = pl.BlockSpec((total, STEP), lambda c, w: (0, c))
    return pl.pallas_call(
        functools.partial(back_kernel, factor),
        out_shape=(
            jax.ShapeDtypeStruct((depth, width), BF),
            jax.ShapeDtypeStruct((depth, width), BF),
            jax.ShapeDtypeStruct((total, depth), BF),
        ),
        grid_spec=pltpu.PrefetchScalarGridSpec(
            num_scalar_prefetch=1,
            grid=(width // STEP,),
            in_specs=[piece] * 8 + [full, full, weight, weight, pl.BlockSpec((depth, total), lambda c, w: (0, 0))],
            out_specs=(weight, weight, pl.BlockSpec((total, depth), lambda c, w: (0, 0))),
            scratch_shapes=[
                pltpu.VMEM((total, STEP), BF),
                pltpu.VMEM((total, STEP), BF),
                pltpu.VMEM((total, depth), F32),
            ],
        ),
        cost_estimate=pl.CostEstimate(
            flops=8 * total * width * depth, bytes_accessed=total * width * 14, transcendentals=0
        ),
    )(where, *ds, slope, active, w_gate, w_up, tok)


def local(tokens, grad_out, gate_pre, up_pre, w_gate, w_up, w_down):
    rows, width = tokens.shape
    factor = float(1.0 / np.sqrt(np.float32(16 * rows)))
    y, zh = lax.axis_index("y"), lax.axis_index("zh")
    p = lax.iota(jnp.int32, 8)
    where = lax.rem(y + p // 2, 4) * 2 + lax.rem(zh + p, 2)

    out_all = gather_col(grad_out)

    g3, g1 = along_y(gate_pre, 1), along_y(gate_pre, -1)
    u3, u1 = along_y(up_pre, 1), along_y(up_pre, -1)
    g2, u2 = along_y(g3, 1), along_y(u1, -1)
    gates = [v for g in (gate_pre, g1, g2, g3) for v in (g, to_pair(g))]
    ups = [v for u in (up_pre, u1, u2, u3) for v in (u, to_pair(u))]

    def part(k):
        here = lax.dynamic_slice_in_dim(out_all, lax.rem(y + k, 4) * (2 * rows), 2 * rows, 0)
        return times_transposed(here, w_down).astype(BF if k else F32)

    recv = [along_y(part(k), k) for k in (2, 1, 3)]
    total = part(0) + sum(r.astype(F32) for r in recv)
    total = total.reshape(2, rows, -1)
    theirs = lax.dynamic_index_in_dim(total, 1 - zh, 0, keepdims=False).astype(BF)
    mine = lax.dynamic_index_in_dim(total, zh, 0, keepdims=False)
    d00 = (mine + to_pair(theirs).astype(F32)).astype(BF)
    d30, d10 = along_y(d00, 1), along_y(d00, -1)
    d01 = to_pair(d00)
    d31, d11 = along_y(d01, 1), along_y(d01, -1)
    d20, d21 = along_y(d30, 1), along_y(d11, -1)
    ds = [d00, d01, d10, d11, d20, d21, d30, d31]

    tok_near = lax.ppermute(tokens, "zl", SWAP)
    zl = lax.axis_index("zl")
    tok_pair = jnp.stack([jnp.where(zl == 0, tokens, tok_near), jnp.where(zl == 0, tok_near, tokens)])
    tok_all = lax.all_to_all(jnp.broadcast_to(tok_pair[None], (4,) + tok_pair.shape), "x", 0, 0, tiled=True)
    tok_turned = tok_all.transpose(3, 1, 0, 2).reshape(width, 8 * rows)

    def both_cores(own):
        other = lax.ppermute(own, "core", SWAP)
        return (own.astype(F32) + other.astype(F32)).astype(BF)

    kept = ()
    for k in (0, 3, 1, 2):
        at = jnp.stack([lax.rem(y + k, 4), zh, 1 - zh]).astype(jnp.int32)
        kept = hidden_of(at, gates[2 * k : 2 * k + 2], ups[2 * k : 2 * k + 2], kept)
    hidden, slope, active = kept
    down = (inner_rows(hidden, out_all) * factor).astype(BF)
    grad_down = both_cores(down)
    gate, up, back = back_of(where, ds, slope, active, w_gate, w_up, tok_turned, factor)
    back_recv = across_col(back.reshape(8, rows, width))
    grad_gate = both_cores(gate)
    grad_up = both_cores(up)
    grad_tokens = jnp.sum(back_recv.astype(F32), axis=0).astype(BF)
    return grad_tokens, grad_gate, grad_up, grad_down


def solution(mesh):
    fine = Mesh(mesh.devices.reshape(4, 2, 2, 4, 2), ("y", "zh", "zl", "x", "core"))
    row, col = ("y", "zh"), COL
    act = P(col + ("core",), row)
    pre = P(row + ("core",), col)
    up = P(row, col)
    down = P(col, row)

    return jax.shard_map(
        local,
        mesh=fine,
        in_specs=(act, act, pre, pre, up, up, down),
        out_specs=(act, up, up, down),
        check_vma=False,
    )
```

```python
import functools

import jax
import jax.numpy as jnp
import numpy as np
from jax import lax
from jax.experimental import pallas as pl
from jax.experimental.pallas import tpu as pltpu
from jax.sharding import Mesh, PartitionSpec as P


COL = ("zl", "x")
BF = jnp.bfloat16
F32 = jnp.float32
SWAP = [(0, 1), (1, 0)]
STEP = 512
NARROW = 256


def ring(shift):
    return [(i, (i + shift) % 4) for i in range(4)]


def along_y(x, shift):
    return lax.ppermute(x, "y", ring(shift))


def to_pair(x):
    return lax.ppermute(x, "zh", SWAP)


def across_col(x):
    return lax.all_to_all(x, COL, 0, 0, tiled=True)


def gather_col(x):
    many = jnp.broadcast_to(x[None], (8,) + x.shape)
    whole = across_col(many)
    return whole.reshape(8 * x.shape[0], x.shape[1])


def inner_rows(left, right):
    return lax.dot_general(left, right, (((0,), (0,)), ((), ())), preferred_element_type=F32)


def times_transposed(left, right):
    return lax.dot_general(left, right, (((1,), (1,)), ((), ())), preferred_element_type=F32)


def place(where, p, rows):
    return pl.ds(pl.multiple_of(where[p] * rows, rows), rows)


def hidden_kernel(at, *refs):
    gates, ups = refs[:2], refs[2:4]
    hidden, slope, active = refs[-3:]
    rows = gates[0].shape[0]
    for j in range(2):
        g = gates[j][...].astype(F32)
        u = ups[j][...].astype(F32)
        s = jax.nn.sigmoid(g)
        here = place(at, 1 + j, rows)
        act = g * s
        hidden[here, :] = (act * u).astype(BF)
        slope[here, :] = u * s * (1.0 + g * (1.0 - s))
        active[here, :] = act


def piece_of(rows, which):
    return pl.BlockSpec((rows, STEP), lambda c, w: (which, c))


def hidden_of(at, rows, gates, ups, before):
    width = gates[0].shape[1]
    total = 8 * rows
    pieces = [piece_of(rows, 0)] * 2 + [piece_of(rows, u.shape[0] // rows - 1) for u in ups]
    pair = pl.BlockSpec((2 * rows, STEP), lambda c, w: (w[0], c))
    kept = [pl.BlockSpec(memory_space=pl.ANY)] * len(before)
    return pl.pallas_call(
        hidden_kernel,
        out_shape=(
            jax.ShapeDtypeStruct((total, width), BF),
            jax.ShapeDtypeStruct((total, width), F32),
            jax.ShapeDtypeStruct((total, width), F32),
        ),
        grid_spec=pltpu.PrefetchScalarGridSpec(
            num_scalar_prefetch=1,
            grid=(width // STEP,),
            in_specs=pieces + kept,
            out_specs=(pair, pair, pair),
        ),
        input_output_aliases={5 + i: i for i in range(len(before))},
        cost_estimate=pl.CostEstimate(
            flops=2 * rows * width * 10, bytes_accessed=2 * rows * width * 14, transcendentals=2 * rows * width * 2
        ),
    )(at, *gates, *ups, *before)


def back_kernel(factor, first, where, *refs):
    ds, refs = refs[:8], refs[8:]
    slope, active, w_gate, w_up, tok = refs[:5]
    grad_gate, grad_up, back, d_gate, d_up, total = refs[-6:]
    rows = ds[0].shape[0]
    c = pl.program_id(0)
    for p in range(8):
        d = ds[p][...].astype(F32)
        here = place(where, p, rows)
        d_gate[here, :] = (d * slope[here, :]).astype(BF)
        d_up[here, :] = (d * active[here, :]).astype(BF)
    dg, du = d_gate[...], d_up[...]
    more = times_transposed(dg, w_gate[...]) + times_transposed(du, w_up[...])
    grad_gate[...] = (jnp.dot(tok[...], dg, preferred_element_type=F32) * factor).astype(BF)
    grad_up[...] = (jnp.dot(tok[...], du, preferred_element_type=F32) * factor).astype(BF)

    @pl.when(c == 0)
    def _():
        total[...] = more if first else refs[5][...] + more

    @pl.when(c > 0)
    def _():
        total[...] += more

    @pl.when(c == pl.num_programs(0) - 1)
    def _():
        back[...] = total[...].astype(back.dtype)


def back_of(where, half, ds, slope, active, w_gate, w_up, tok, factor, before):
    rows, part = ds[0].shape
    depth, width = w_gate.shape
    total = 8 * rows
    steps = part // NARROW
    piece = pl.BlockSpec((rows, NARROW), lambda c, w: (0, c))
    weight = pl.BlockSpec((depth, NARROW), lambda c, w: (0, c + half * steps))
    full = pl.BlockSpec((total, NARROW), lambda c, w: (0, c + half * steps))
    whole = pl.BlockSpec((total, depth), lambda c, w: (0, 0))
    kept = [whole] + [pl.BlockSpec(memory_space=pl.ANY)] * 2 if before else []
    return pl.pallas_call(
        functools.partial(back_kernel, factor, not before),
        out_shape=(
            jax.ShapeDtypeStruct((depth, width), BF),
            jax.ShapeDtypeStruct((depth, width), BF),
            jax.ShapeDtypeStruct((total, depth), BF if before else F32),
        ),
        grid_spec=pltpu.PrefetchScalarGridSpec(
            num_scalar_prefetch=1,
            grid=(steps,),
            in_specs=[piece] * 8
            + [full, full, weight, weight, pl.BlockSpec((depth, total), lambda c, w: (0, 0))]
            + kept,
            out_specs=(weight, weight, whole),
            scratch_shapes=[
                pltpu.VMEM((total, NARROW), BF),
                pltpu.VMEM((total, NARROW), BF),
                pltpu.VMEM((total, depth), F32),
            ],
        ),
        input_output_aliases={15: 0, 16: 1} if before else {},
        cost_estimate=pl.CostEstimate(
            flops=8 * total * part * depth, bytes_accessed=total * part * 14, transcendentals=0
        ),
    )(where, *ds, slope, active, w_gate, w_up, tok, *before)


def local(tokens, grad_out, gate_pre, up_pre, w_gate, w_up, w_down):
    rows, width = tokens.shape
    factor = float(1.0 / np.sqrt(np.float32(16 * rows)))
    y, zh = lax.axis_index("y"), lax.axis_index("zh")
    p = lax.iota(jnp.int32, 8)
    where = lax.rem(y + p // 2, 4) * 2 + lax.rem(zh + p, 2)

    out_all = gather_col(grad_out)

    both = jnp.concatenate([gate_pre, up_pre], axis=0)
    both3, both1 = along_y(both, 1), along_y(both, -1)
    g2 = along_y(both3[:rows], 1)
    u2 = along_y(both1[rows:], -1)
    paired = {k: (v, to_pair(v)) for k, v in ((0, both), (3, both3), (1, both1))}
    saved = {k: (v, v) for k, v in paired.items()}
    saved[2] = ((g2, to_pair(g2)), (u2, to_pair(u2)))

    part_rows = w_down.shape[0] // 2

    def part(h, k):
        here = lax.dynamic_slice_in_dim(out_all, lax.rem(y + k, 4) * (2 * rows), 2 * rows, 0)
        return times_transposed(here, w_down[h * part_rows : (h + 1) * part_rows]).astype(BF if k else F32)

    def gathered(h):
        recv = [along_y(part(h, k), k) for k in (2, 1, 3)]
        total = part(h, 0) + sum(r.astype(F32) for r in recv)
        total = total.reshape(2, rows, -1)
        theirs = lax.dynamic_index_in_dim(total, 1 - zh, 0, keepdims=False).astype(BF)
        mine = lax.dynamic_index_in_dim(total, zh, 0, keepdims=False)
        d00 = (mine + to_pair(theirs).astype(F32)).astype(BF)
        d30, d10 = along_y(d00, 1), along_y(d00, -1)
        d01 = to_pair(d00)
        d31, d11 = along_y(d01, 1), along_y(d01, -1)
        d20, d21 = along_y(d30, 1), along_y(d11, -1)
        return [d00, d01, d10, d11, d20, d21, d30, d31]

    halves = [gathered(h) for h in (0, 1)]

    tok_near = lax.ppermute(tokens, "zl", SWAP)
    zl = lax.axis_index("zl")
    tok_pair = jnp.stack([jnp.where(zl == 0, tokens, tok_near), jnp.where(zl == 0, tok_near, tokens)])
    tok_all = lax.all_to_all(jnp.broadcast_to(tok_pair[None], (4,) + tok_pair.shape), "x", 0, 0, tiled=True)
    tok_turned = tok_all.transpose(3, 1, 0, 2).reshape(width, 8 * rows)

    def both_cores(own):
        other = lax.ppermute(own, "core", SWAP)
        return (own.astype(F32) + other.astype(F32)).astype(BF)

    kept = ()
    for k in (0, 3, 1, 2):
        at = jnp.stack([lax.rem(y + k, 4), zh, 1 - zh]).astype(jnp.int32)
        kept = hidden_of(at, rows, *saved[k], kept)
    hidden, slope, active = kept
    down = (inner_rows(hidden, out_all) * factor).astype(BF)
    grad_down = both_cores(down)
    before = ()
    for h in (0, 1):
        gate, up, back = back_of(where, h, halves[h], slope, active, w_gate, w_up, tok_turned, factor, before)
        before = (back, gate, up)
    back_recv = across_col(back.reshape(8, rows, width))
    grad_gate = both_cores(gate)
    grad_up = both_cores(up)
    grad_tokens = jnp.sum(back_recv.astype(F32), axis=0).astype(BF)
    return grad_tokens, grad_gate, grad_up, grad_down


def solution(mesh):
    fine = Mesh(mesh.devices.reshape(4, 2, 2, 4, 2), ("y", "zh", "zl", "x", "core"))
    row, col = ("y", "zh"), COL
    act = P(col + ("core",), row)
    pre = P(row + ("core",), col)
    up = P(row, col)
    down = P(col, row)

    return jax.shard_map(
        local,
        mesh=fine,
        in_specs=(act, act, pre, pre, up, up, down),
        out_specs=(act, up, up, down),
        check_vma=False,
    )
```

```python
import functools

import jax
import jax.numpy as jnp
import numpy as np
from jax import lax
from jax.experimental import pallas as pl
from jax.experimental.pallas import tpu as pltpu
from jax.sharding import Mesh, PartitionSpec as P


COL = ("zl", "x")
BF = jnp.bfloat16
F32 = jnp.float32
SWAP = [(0, 1), (1, 0)]
STEP = 512
NARROW = 256


def ring(shift):
    return [(i, (i + shift) % 4) for i in range(4)]


def along_y(x, shift):
    return lax.ppermute(x, "y", ring(shift))


def to_pair(x):
    return lax.ppermute(x, "zh", SWAP)


def across_col(x):
    return lax.all_to_all(x, COL, 0, 0, tiled=True)


def gather_col(x):
    many = jnp.broadcast_to(x[None], (8,) + x.shape)
    whole = across_col(many)
    return whole.reshape(8 * x.shape[0], x.shape[1])


def inner_rows(left, right):
    return lax.dot_general(left, right, (((0,), (0,)), ((), ())), preferred_element_type=F32)


def times_transposed(left, right):
    return lax.dot_general(left, right, (((1,), (1,)), ((), ())), preferred_element_type=F32)


def place(where, p, rows):
    return pl.ds(pl.multiple_of(where[p] * rows, rows), rows)


def hidden_kernel(spots, *refs):
    gates, ups = refs[:2], refs[2:4]
    hidden, slope, active = refs[-3:]
    rows = gates[0].shape[0]
    for j in range(2):
        g = gates[j][...].astype(F32)
        u = ups[j][...].astype(F32)
        s = 0.5 * jnp.tanh(0.5 * g) + 0.5
        here = place(spots, 4 + j, rows)
        act = g * s
        hidden[here, :] = (act * u).astype(BF)
        slope[here, :] = u * s * (1.0 + g * (1.0 - s))
        active[here, :] = act


def piece_of(rows, which):
    return pl.BlockSpec((rows, STEP), lambda c, w: (which, c))


def hidden_of(spots, k, rows, gates, ups, before):
    width = gates[0].shape[1]
    total = 8 * rows
    pieces = [piece_of(rows, 0)] * 2 + [piece_of(rows, u.shape[0] // rows - 1) for u in ups]
    pair = pl.BlockSpec((2 * rows, STEP), lambda c, w: (w[k], c))
    kept = [pl.BlockSpec(memory_space=pl.ANY)] * len(before)
    return pl.pallas_call(
        hidden_kernel,
        out_shape=(
            jax.ShapeDtypeStruct((total, width), BF),
            jax.ShapeDtypeStruct((total, width), F32),
            jax.ShapeDtypeStruct((total, width), F32),
        ),
        grid_spec=pltpu.PrefetchScalarGridSpec(
            num_scalar_prefetch=1,
            grid=(width // STEP,),
            in_specs=pieces + kept,
            out_specs=(pair, pair, pair),
        ),
        input_output_aliases={5 + i: i for i in range(len(before))},
        cost_estimate=pl.CostEstimate(
            flops=2 * rows * width * 10, bytes_accessed=2 * rows * width * 14, transcendentals=2 * rows * width * 2
        ),
    )(spots, *gates, *ups, *before)


def back_kernel(factor, first, spots, *refs):
    ds, refs = refs[:5], refs[5:]
    slope, active, w_gate, w_up, tok = refs[:5]
    grad_gate, grad_up, back, d_gate, d_up, total = refs[-6:]
    c = pl.program_id(0)
    for ref, k, skip in zip(ds, (0, 1, 3, 2, 2), (0, 0, 0, 0, 1)):
        d = ref[...].astype(F32)
        rows = d.shape[0]
        here = pl.ds(pl.multiple_of(spots[k] * ds[0].shape[0] + skip * rows, rows), rows)
        d_gate[here, :] = (d * slope[here, :]).astype(BF)
        d_up[here, :] = (d * active[here, :]).astype(BF)
    dg, du = d_gate[...], d_up[...]
    more = times_transposed(dg, w_gate[...]) + times_transposed(du, w_up[...])
    grad_gate[...] = (jnp.dot(tok[...], dg, preferred_element_type=F32) * factor).astype(BF)
    grad_up[...] = (jnp.dot(tok[...], du, preferred_element_type=F32) * factor).astype(BF)

    @pl.when(c == 0)
    def _():
        total[...] = more if first else refs[5][...] + more

    @pl.when(c > 0)
    def _():
        total[...] += more

    @pl.when(c == pl.num_programs(0) - 1)
    def _():
        back[...] = total[...].astype(back.dtype)


def back_of(spots, half, ds, slope, active, w_gate, w_up, tok, factor, before):
    rows, part = ds[0].shape
    depth, width = w_gate.shape
    total = 4 * rows
    steps = part // NARROW
    pieces = [pl.BlockSpec((d.shape[0], NARROW), lambda c, w: (0, c)) for d in ds]
    weight = pl.BlockSpec((depth, NARROW), lambda c, w: (0, c + half * steps))
    full = pl.BlockSpec((total, NARROW), lambda c, w: (0, c + half * steps))
    whole = pl.BlockSpec((total, depth), lambda c, w: (0, 0))
    kept = [whole] + [pl.BlockSpec(memory_space=pl.ANY)] * 2 if before else []
    return pl.pallas_call(
        functools.partial(back_kernel, factor, not before),
        out_shape=(
            jax.ShapeDtypeStruct((depth, width), BF),
            jax.ShapeDtypeStruct((depth, width), BF),
            jax.ShapeDtypeStruct((total, depth), BF if before else F32),
        ),
        grid_spec=pltpu.PrefetchScalarGridSpec(
            num_scalar_prefetch=1,
            grid=(steps,),
            in_specs=pieces
            + [full, full, weight, weight, pl.BlockSpec((depth, total), lambda c, w: (0, 0))]
            + kept,
            out_specs=(weight, weight, whole),
            scratch_shapes=[
                pltpu.VMEM((total, NARROW), BF),
                pltpu.VMEM((total, NARROW), BF),
                pltpu.VMEM((total, depth), F32),
            ],
        ),
        input_output_aliases={12: 0, 13: 1} if before else {},
        cost_estimate=pl.CostEstimate(
            flops=8 * total * part * depth, bytes_accessed=total * part * 14, transcendentals=0
        ),
    )(spots, *ds, slope, active, w_gate, w_up, tok, *before)


def local(tokens, grad_out, gate_pre, up_pre, w_gate, w_up, w_down):
    rows, width = tokens.shape
    factor = float(1.0 / np.sqrt(np.float32(16 * rows)))
    y, zh = lax.axis_index("y"), lax.axis_index("zh")
    p = lax.iota(jnp.int32, 6)
    spots = jnp.where(p < 4, lax.rem(y + p, 4), jnp.where(p == 4, zh, 1 - zh))

    out_all = gather_col(grad_out)

    both = jnp.concatenate([gate_pre, up_pre], axis=0)
    both3, both1 = along_y(both, 1), along_y(both, -1)
    g2 = along_y(both3[:rows], 1)
    u2 = along_y(both1[rows:], -1)
    paired = {k: (v, to_pair(v)) for k, v in ((0, both), (3, both3), (1, both1))}
    saved = {k: (v, v) for k, v in paired.items()}
    saved[2] = ((g2, to_pair(g2)), (u2, to_pair(u2)))

    part_rows = w_down.shape[0] // 2

    def gathered(h):
        part = times_transposed(out_all, w_down[h * part_rows : (h + 1) * part_rows]).astype(BF)
        recv = lax.all_to_all(part.reshape(4, 2 * rows, part_rows), "y", 0, 0, tiled=True)
        total = jnp.sum(recv.astype(F32), axis=0)
        mine = total.astype(BF)
        d = (total + to_pair(mine).astype(F32)).astype(BF)
        d3, d1 = along_y(d, 1), along_y(d, -1)
        return [d, d1, d3, along_y(d3[:rows], 1), along_y(d1[rows:], -1)]

    halves = [gathered(h) for h in (0, 1)]

    tok_near = lax.ppermute(tokens, "zl", SWAP)
    zl = lax.axis_index("zl")
    tok_pair = jnp.stack([jnp.where(zl == 0, tokens, tok_near), jnp.where(zl == 0, tok_near, tokens)])
    tok_all = lax.all_to_all(jnp.broadcast_to(tok_pair[None], (4,) + tok_pair.shape), "x", 0, 0, tiled=True)
    tok_turned = tok_all.transpose(3, 1, 0, 2).reshape(width, 8 * rows)

    def both_cores(own):
        other = lax.ppermute(own, "core", SWAP)
        return (own.astype(F32) + other.astype(F32)).astype(BF)

    kept = ()
    for k in (0, 3, 1, 2):
        kept = hidden_of(spots, k, rows, *saved[k], kept)
    hidden, slope, active = kept
    down = (inner_rows(hidden, out_all) * factor).astype(BF)
    grad_down = both_cores(down)
    before = ()
    for h in (0, 1):
        gate, up, back = back_of(spots, h, halves[h], slope, active, w_gate, w_up, tok_turned, factor, before)
        before = (back, gate, up)
    back_recv = across_col(back.reshape(8, rows, width))
    grad_gate = both_cores(gate)
    grad_up = both_cores(up)
    grad_tokens = jnp.sum(back_recv.astype(F32), axis=0).astype(BF)
    return grad_tokens, grad_gate, grad_up, grad_down


def solution(mesh):
    fine = Mesh(mesh.devices.reshape(4, 2, 2, 4, 2), ("y", "zh", "zl", "x", "core"))
    row, col = ("y", "zh"), COL
    act = P(col + ("core",), row)
    pre = P(row + ("core",), col)
    up = P(row, col)
    down = P(col, row)

    return jax.shard_map(
        local,
        mesh=fine,
        in_specs=(act, act, pre, pre, up, up, down),
        out_specs=(act, up, up, down),
        check_vma=False,
    )
```

```python
import functools

import jax
import jax.numpy as jnp
import numpy as np
from jax import lax
from jax.experimental import pallas as pl
from jax.experimental.pallas import tpu as pltpu
from jax.sharding import Mesh, PartitionSpec as P


COL = ("zl", "x")
BF = jnp.bfloat16
F32 = jnp.float32
SWAP = [(0, 1), (1, 0)]
STEP = 256


def ring(shift):
    return [(i, (i + shift) % 4) for i in range(4)]


def along_y(x, shift):
    return lax.ppermute(x, "y", ring(shift))


def to_pair(x):
    return lax.ppermute(x, "zh", SWAP)


def across_col(x):
    return lax.all_to_all(x, COL, 0, 0, tiled=True)


def gather_col(x):
    many = jnp.broadcast_to(x[None], (8,) + x.shape)
    whole = across_col(many)
    return whole.reshape(8 * x.shape[0], x.shape[1])


def inner_rows(left, right):
    return lax.dot_general(left, right, (((0,), (0,)), ((), ())), preferred_element_type=F32)


def times_transposed(left, right):
    return lax.dot_general(left, right, (((1,), (1,)), ((), ())), preferred_element_type=F32)


def rows_at(block, rows):
    return pl.ds(pl.multiple_of(block * rows, rows), rows)


def back_kernel(factor, first, rows, spots, *refs):
    gates, ups, ds, refs = refs[:8], refs[8:16], refs[16:21], refs[21:]
    w_gate, w_up, tok, out = refs[:4]
    grad_gate, grad_up, grad_down, back, hidden, d_gate, d_up, total, tokens = refs[-9:]
    c = pl.program_id(0)
    flip = spots[4] == 1

    @pl.when(c == 0)
    def _():
        for b in range(8):
            tokens[:, b * rows : (b + 1) * rows] = tok[b]

    for k in range(4):
        for j in range(2):
            here = rows_at(2 * spots[k] + spots[4 + j], rows)
            g = gates[2 * k + j][...].astype(F32)
            u = ups[2 * k + j][...].astype(F32)
            if k == 2:
                low, high = ds[3][...].astype(F32), ds[4][...].astype(F32)
                d = jnp.where(flip, high, low) if j == 0 else jnp.where(flip, low, high)
            else:
                d = ds[(0, 1, None, 2)[k]][rows_at(spots[4 + j], rows), :].astype(F32)
            s = 0.5 * jnp.tanh(0.5 * g) + 0.5
            active = g * s
            hidden[here, :] = (active * u).astype(BF)
            d_gate[here, :] = (d * u * s * (1.0 + g * (1.0 - s))).astype(BF)
            d_up[here, :] = (d * active).astype(BF)
    dg, du = d_gate[...], d_up[...]
    more = times_transposed(dg, w_gate[...]) + times_transposed(du, w_up[...])
    grad_gate[...] = (jnp.dot(tokens[...], dg, preferred_element_type=F32) * factor).astype(BF)
    grad_up[...] = (jnp.dot(tokens[...], du, preferred_element_type=F32) * factor).astype(BF)
    grad_down[...] = (inner_rows(hidden[...], out[...]) * factor).astype(BF)

    @pl.when(c == 0)
    def _():
        total[...] = more if first else refs[4][...] + more

    @pl.when(c > 0)
    def _():
        total[...] += more

    @pl.when(c == pl.num_programs(0) - 1)
    def _():
        back[...] = total[...].astype(back.dtype)


def back_of(spots, half, saved, ds, w_gate, w_up, tok, out, factor, before):
    depth, width = w_gate.shape
    rows = tok.shape[2]
    part = ds[0].shape[1]
    total = 8 * rows
    steps = part // STEP
    gates = [v for k in range(4) for v in saved[k][0]]
    ups = [v for k in range(4) for v in saved[k][1]]

    def piece(v, which):
        return pl.BlockSpec((rows, STEP), lambda c, w: (which * (v.shape[0] // rows - 1), c + half * steps))

    d_specs = [pl.BlockSpec((d.shape[0], STEP), lambda c, w: (0, c)) for d in ds]
    weight = pl.BlockSpec((depth, STEP), lambda c, w: (0, c + half * steps))
    down = pl.BlockSpec((STEP, depth), lambda c, w: (c + half * steps, 0))
    whole = pl.BlockSpec((total, depth), lambda c, w: (0, 0))
    kept = [whole] + [pl.BlockSpec(memory_space=pl.ANY)] * 3 if before else []
    return pl.pallas_call(
        functools.partial(back_kernel, factor, not before, rows),
        out_shape=(
            jax.ShapeDtypeStruct((depth, width), BF),
            jax.ShapeDtypeStruct((depth, width), BF),
            jax.ShapeDtypeStruct((width, depth), BF),
            jax.ShapeDtypeStruct((total, depth), BF if before else F32),
        ),
        grid_spec=pltpu.PrefetchScalarGridSpec(
            num_scalar_prefetch=1,
            grid=(steps,),
            in_specs=[piece(v, 0) for v in gates]
            + [piece(v, 1) for v in ups]
            + d_specs
            + [weight, weight, pl.BlockSpec(tok.shape, lambda c, w: (0, 0, 0)), whole]
            + kept,
            out_specs=(weight, weight, down, whole),
            scratch_shapes=[pltpu.VMEM((total, STEP), BF)] * 3
            + [pltpu.VMEM((total, depth), F32), pltpu.VMEM((depth, total), BF)],
        ),
        input_output_aliases={27: 0, 28: 1, 29: 2} if before else {},
        cost_estimate=pl.CostEstimate(
            flops=10 * total * part * depth, bytes_accessed=total * part * 16, transcendentals=total * part
        ),
    )(spots, *gates, *ups, *ds, w_gate, w_up, tok, out, *before)


def local(tokens, grad_out, gate_pre, up_pre, w_gate, w_up, w_down):
    rows, width = tokens.shape
    factor = float(1.0 / np.sqrt(np.float32(16 * rows)))
    y, zh = lax.axis_index("y"), lax.axis_index("zh")
    p = lax.iota(jnp.int32, 6)
    spots = jnp.where(p < 4, lax.rem(y + p, 4), jnp.where(p == 4, zh, 1 - zh))

    out_all = gather_col(grad_out)

    both = jnp.concatenate([gate_pre, up_pre], axis=0)
    both3, both1 = along_y(both, 1), along_y(both, -1)
    g2 = along_y(both3[:rows], 1)
    u2 = along_y(both1[rows:], -1)
    paired = {k: (v, to_pair(v)) for k, v in ((0, both), (3, both3), (1, both1))}
    saved = {k: (v, v) for k, v in paired.items()}
    saved[2] = ((g2, to_pair(g2)), (u2, to_pair(u2)))

    part_rows = w_down.shape[0] // 2

    def gathered(h):
        part = times_transposed(out_all, w_down[h * part_rows : (h + 1) * part_rows]).astype(BF)
        recv = lax.all_to_all(part.reshape(4, 2 * rows, part_rows), "y", 0, 0, tiled=True)
        total = jnp.sum(recv.astype(F32), axis=0)
        mine = total.astype(BF)
        d = (total + to_pair(mine).astype(F32)).astype(BF)
        d3, d1 = along_y(d, 1), along_y(d, -1)
        return [d, d1, d3, along_y(d3[:rows], 1), along_y(d1[rows:], -1)]

    halves = [gathered(h) for h in (0, 1)]

    turned = tokens.T
    turned = jnp.broadcast_to(turned[None], (8, width, rows))
    tok_all = across_col(turned)

    def both_cores(own):
        other = lax.ppermute(own, "core", SWAP)
        return (own.astype(F32) + other.astype(F32)).astype(BF)

    before = ()
    for h in (0, 1):
        gate, up, down, back = back_of(
            spots, h, saved, halves[h], w_gate, w_up, tok_all, out_all, factor, before
        )
        before = (back, gate, up, down)
    back_recv = across_col(back.reshape(8, rows, width))
    grad_down = both_cores(down)
    grad_gate = both_cores(gate)
    grad_up = both_cores(up)
    grad_tokens = jnp.sum(back_recv.astype(F32), axis=0).astype(BF)
    return grad_tokens, grad_gate, grad_up, grad_down


def solution(mesh):
    fine = Mesh(mesh.devices.reshape(4, 2, 2, 4, 2), ("y", "zh", "zl", "x", "core"))
    row, col = ("y", "zh"), COL
    act = P(col + ("core",), row)
    pre = P(row + ("core",), col)
    up = P(row, col)
    down = P(col, row)

    return jax.shard_map(
        local,
        mesh=fine,
        in_specs=(act, act, pre, pre, up, up, down),
        out_specs=(act, up, up, down),
        check_vma=False,
    )
```

```python
import functools

import jax
import jax.numpy as jnp
import numpy as np
from jax import lax
from jax.experimental import pallas as pl
from jax.experimental.pallas import tpu as pltpu
from jax.sharding import Mesh, PartitionSpec as P


COL = ("zl", "x")
BF = jnp.bfloat16
F32 = jnp.float32
SWAP = [(0, 1), (1, 0)]
STEP = 512
NARROW = 256


def ring(shift):
    return [(i, (i + shift) % 4) for i in range(4)]


def along_y(x, shift):
    return lax.ppermute(x, "y", ring(shift))


def to_pair(x):
    return lax.ppermute(x, "zh", SWAP)


def across_col(x):
    return lax.all_to_all(x, COL, 0, 0, tiled=True)


def gather_col(x):
    many = jnp.broadcast_to(x[None], (8,) + x.shape)
    whole = across_col(many)
    return whole.reshape(8 * x.shape[0], x.shape[1])


def inner_rows(left, right):
    return lax.dot_general(left, right, (((0,), (0,)), ((), ())), preferred_element_type=F32)


def times_transposed(left, right):
    return lax.dot_general(left, right, (((1,), (1,)), ((), ())), preferred_element_type=F32)


def place(where, p, rows):
    return pl.ds(pl.multiple_of(where[p] * rows, rows), rows)


def hidden_kernel(spots, *refs):
    gates, ups = refs[:2], refs[2:4]
    hidden, slope, active = refs[-3:]
    rows = gates[0].shape[0]
    for j in range(2):
        g = gates[j][...].astype(F32)
        u = ups[j][...].astype(F32)
        s = 0.5 * jnp.tanh(0.5 * g) + 0.5
        here = place(spots, 4 + j, rows)
        act = g * s
        hidden[here, :] = (act * u).astype(BF)
        slope[here, :] = u * s * (1.0 + g * (1.0 - s))
        active[here, :] = act


def piece_of(rows, which):
    return pl.BlockSpec((rows, STEP), lambda c, w: (which, c))


def hidden_of(spots, k, rows, gates, ups, before):
    width = gates[0].shape[1]
    total = 8 * rows
    pieces = [piece_of(rows, 0)] * 2 + [piece_of(rows, u.shape[0] // rows - 1) for u in ups]
    pair = pl.BlockSpec((2 * rows, STEP), lambda c, w: (w[k], c))
    kept = [pl.BlockSpec(memory_space=pl.ANY)] * len(before)
    return pl.pallas_call(
        hidden_kernel,
        out_shape=(
            jax.ShapeDtypeStruct((total, width), BF),
            jax.ShapeDtypeStruct((total, width), F32),
            jax.ShapeDtypeStruct((total, width), F32),
        ),
        grid_spec=pltpu.PrefetchScalarGridSpec(
            num_scalar_prefetch=1,
            grid=(width // STEP,),
            in_specs=pieces + kept,
            out_specs=(pair, pair, pair),
        ),
        input_output_aliases={5 + i: i for i in range(len(before))},
        cost_estimate=pl.CostEstimate(
            flops=2 * rows * width * 10, bytes_accessed=2 * rows * width * 14, transcendentals=2 * rows * width * 2
        ),
    )(spots, *gates, *ups, *before)


def back_kernel(factor, first, spots, *refs):
    ds, refs = refs[:5], refs[5:]
    slope, active, w_gate, w_up = refs[:4]
    toks, refs = refs[4:8], refs[8:]
    grad_gate, grad_up, back, d_gate, d_up, total, tokens = refs[-7:]
    c = pl.program_id(0)

    @pl.when(c == 0)
    def _():
        depth, wide = tokens.shape[0], toks[0].shape[1]
        for m in range(4):
            for j in range(2):
                here = pl.ds(pl.multiple_of(spots[6 + 2 * m + j] * wide, wide), wide)
                tokens[:, here] = toks[m][j * depth : (j + 1) * depth, :]

    for ref, k, skip in zip(ds, (0, 1, 3, 2, 2), (0, 0, 0, 0, 1)):
        d = ref[...].astype(F32)
        rows = d.shape[0]
        here = pl.ds(pl.multiple_of(spots[k] * ds[0].shape[0] + skip * rows, rows), rows)
        d_gate[here, :] = (d * slope[here, :]).astype(BF)
        d_up[here, :] = (d * active[here, :]).astype(BF)
    dg, du = d_gate[...], d_up[...]
    more = times_transposed(dg, w_gate[...]) + times_transposed(du, w_up[...])
    grad_gate[...] = (jnp.dot(tokens[...], dg, preferred_element_type=F32) * factor).astype(BF)
    grad_up[...] = (jnp.dot(tokens[...], du, preferred_element_type=F32) * factor).astype(BF)

    @pl.when(c == 0)
    def _():
        total[...] = more if first else refs[0][...] + more

    @pl.when(c > 0)
    def _():
        total[...] += more

    @pl.when(c == pl.num_programs(0) - 1)
    def _():
        back[...] = total[...].astype(back.dtype)


def back_of(spots, half, ds, slope, active, w_gate, w_up, toks, factor, before):
    rows, part = ds[0].shape
    depth, width = w_gate.shape
    total = 4 * rows
    steps = part // NARROW
    pieces = [pl.BlockSpec((d.shape[0], NARROW), lambda c, w: (0, c)) for d in ds]
    weight = pl.BlockSpec((depth, NARROW), lambda c, w: (0, c + half * steps))
    full = pl.BlockSpec((total, NARROW), lambda c, w: (0, c + half * steps))
    whole = pl.BlockSpec((total, depth), lambda c, w: (0, 0))
    kept = [whole] + [pl.BlockSpec(memory_space=pl.ANY)] * 2 if before else []
    return pl.pallas_call(
        functools.partial(back_kernel, factor, not before),
        out_shape=(
            jax.ShapeDtypeStruct((depth, width), BF),
            jax.ShapeDtypeStruct((depth, width), BF),
            jax.ShapeDtypeStruct((total, depth), BF if before else F32),
        ),
        grid_spec=pltpu.PrefetchScalarGridSpec(
            num_scalar_prefetch=1,
            grid=(steps,),
            in_specs=pieces
            + [full, full, weight, weight]
            + [pl.BlockSpec(t.shape, lambda c, w: (0, 0)) for t in toks]
            + kept,
            out_specs=(weight, weight, whole),
            scratch_shapes=[
                pltpu.VMEM((total, NARROW), BF),
                pltpu.VMEM((total, NARROW), BF),
                pltpu.VMEM((total, depth), F32),
                pltpu.VMEM((depth, total), BF),
            ],
        ),
        input_output_aliases={15: 0, 16: 1} if before else {},
        cost_estimate=pl.CostEstimate(
            flops=8 * total * part * depth, bytes_accessed=total * part * 14, transcendentals=0
        ),
    )(spots, *ds, slope, active, w_gate, w_up, *toks, *before)


def local(tokens, grad_out, gate_pre, up_pre, w_gate, w_up, w_down):
    rows, width = tokens.shape
    factor = float(1.0 / np.sqrt(np.float32(16 * rows)))
    y, zh = lax.axis_index("y"), lax.axis_index("zh")
    x, zl = lax.axis_index("x"), lax.axis_index("zl")
    p = lax.iota(jnp.int32, 14)
    spots = jnp.where(p < 4, lax.rem(y + p, 4), jnp.where(p == 4, zh, 1 - zh))
    m = p - 6
    far = jnp.where(lax.rem(m, 2) == 0, zl, 1 - zl) * 4 + lax.rem(x + m // 2, 4)
    spots = jnp.where(p < 6, spots, far)

    out_all = gather_col(grad_out)

    both = jnp.concatenate([gate_pre, up_pre], axis=0)
    both3, both1 = along_y(both, 1), along_y(both, -1)
    low3 = both3[:rows]
    high1 = both1[rows:]
    g2, u2 = along_y(low3, 1), along_y(high1, -1)
    paired = {k: (v, to_pair(v)) for k, v in ((0, both), (3, both3), (1, both1))}
    saved = {k: (v, v) for k, v in paired.items()}
    saved[2] = ((g2, along_y(paired[3][1][:rows], 1)), (u2, along_y(paired[1][1][rows:], -1)))

    part_rows = w_down.shape[0] // 2

    def gathered(h):
        part = times_transposed(out_all, w_down[h * part_rows : (h + 1) * part_rows]).astype(BF)
        recv = lax.all_to_all(part.reshape(4, 2 * rows, part_rows), "y", 0, 0, tiled=True)
        total = jnp.sum(recv.astype(F32), axis=0)
        mine = total.astype(BF)
        d = (total + to_pair(mine).astype(F32)).astype(BF)
        d3, d1 = along_y(d, 1), along_y(d, -1)
        return [d, d1, d3, along_y(d3[:rows], 1), along_y(d1[rows:], -1)]

    halves = [gathered(h) for h in (0, 1)]

    turned = tokens.T
    near = lax.ppermute(turned, "zl", SWAP)
    pair = jnp.concatenate([turned, near], axis=0)
    toks = [pair]
    for m in (1, 2, 3):
        toks.append(lax.ppermute(pair, "x", ring(-m)))

    def both_cores(own):
        other = lax.ppermute(own, "core", SWAP)
        return (own.astype(F32) + other.astype(F32)).astype(BF)

    kept = ()
    for k in (0, 3, 1, 2):
        kept = hidden_of(spots, k, rows, *saved[k], kept)
    hidden, slope, active = kept
    down = (inner_rows(hidden, out_all) * factor).astype(BF)
    grad_down = both_cores(down)
    before = ()
    for h in (0, 1):
        gate, up, back = back_of(spots, h, halves[h], slope, active, w_gate, w_up, toks, factor, before)
        before = (back, gate, up)
    back_recv = across_col(back.reshape(8, rows, width))
    grad_gate = both_cores(gate)
    grad_up = both_cores(up)
    grad_tokens = jnp.sum(back_recv.astype(F32), axis=0).astype(BF)
    return grad_tokens, grad_gate, grad_up, grad_down


def solution(mesh):
    fine = Mesh(mesh.devices.reshape(4, 2, 2, 4, 2), ("y", "zh", "zl", "x", "core"))
    row, col = ("y", "zh"), COL
    act = P(col + ("core",), row)
    pre = P(row + ("core",), col)
    up = P(row, col)
    down = P(col, row)

    return jax.shard_map(
        local,
        mesh=fine,
        in_specs=(act, act, pre, pre, up, up, down),
        out_specs=(act, up, up, down),
        check_vma=False,
    )
```

```python
import functools

import jax
import jax.numpy as jnp
import numpy as np
from jax import lax
from jax.experimental import pallas as pl
from jax.experimental.pallas import tpu as pltpu
from jax.sharding import Mesh, PartitionSpec as P


COL = ("zl", "x")
BF = jnp.bfloat16
F32 = jnp.float32
SWAP = [(0, 1), (1, 0)]
STEP = 512
NARROW = 256


def ring(shift):
    return [(i, (i + shift) % 4) for i in range(4)]


def along_y(x, shift):
    return lax.ppermute(x, "y", ring(shift))


def to_pair(x):
    return lax.ppermute(x, "zh", SWAP)


def across_col(x):
    return lax.all_to_all(x, COL, 0, 0, tiled=True)


def gather_col(x):
    many = jnp.broadcast_to(x[None], (8,) + x.shape)
    whole = across_col(many)
    return whole.reshape(8 * x.shape[0], x.shape[1])


def inner_rows(left, right):
    return lax.dot_general(left, right, (((0,), (0,)), ((), ())), preferred_element_type=F32)


def times_transposed(left, right):
    return lax.dot_general(left, right, (((1,), (1,)), ((), ())), preferred_element_type=F32)


def place(where, p, rows):
    return pl.ds(pl.multiple_of(where[p] * rows, rows), rows)


def hidden_kernel(spots, *refs):
    gates, ups = refs[:2], refs[2:4]
    hidden, slope, active = refs[-3:]
    rows = gates[0].shape[0]
    for j in range(2):
        g = gates[j][...].astype(F32)
        u = ups[j][...].astype(F32)
        s = 0.5 * jnp.tanh(0.5 * g) + 0.5
        here = place(spots, 4 + j, rows)
        act = g * s
        hidden[here, :] = (act * u).astype(BF)
        slope[here, :] = u * s * (1.0 + g * (1.0 - s))
        active[here, :] = act


def piece_of(rows, which):
    return pl.BlockSpec((rows, STEP), lambda c, w: (which, c))


def hidden_of(spots, k, rows, gates, ups, before):
    width = gates[0].shape[1]
    total = 8 * rows
    pieces = [piece_of(rows, 0)] * 2 + [piece_of(rows, u.shape[0] // rows - 1) for u in ups]
    pair = pl.BlockSpec((2 * rows, STEP), lambda c, w: (w[k], c))
    kept = [pl.BlockSpec(memory_space=pl.ANY)] * len(before)
    return pl.pallas_call(
        hidden_kernel,
        out_shape=(
            jax.ShapeDtypeStruct((total, width), BF),
            jax.ShapeDtypeStruct((total, width), F32),
            jax.ShapeDtypeStruct((total, width), F32),
        ),
        grid_spec=pltpu.PrefetchScalarGridSpec(
            num_scalar_prefetch=1,
            grid=(width // STEP,),
            in_specs=pieces + kept,
            out_specs=(pair, pair, pair),
        ),
        input_output_aliases={5 + i: i for i in range(len(before))},
        cost_estimate=pl.CostEstimate(
            flops=2 * rows * width * 10, bytes_accessed=2 * rows * width * 14, transcendentals=2 * rows * width * 2
        ),
    )(spots, *gates, *ups, *before)


def back_kernel(factor, first, spots, *refs):
    ds, refs = refs[:5], refs[5:]
    slope, active, w_gate, w_up = refs[:4]
    toks, refs = refs[4:8], refs[8:]
    grad_gate, grad_up, back, both, weights, total, tokens = refs[-7:]
    c = pl.program_id(0)

    @pl.when(c == 0)
    def _():
        total[...] = jnp.zeros_like(total) if first else refs[0][...]
        depth, wide = tokens.shape[0], toks[0].shape[1]
        for m in range(4):
            for j in range(2):
                here = pl.ds(pl.multiple_of(spots[6 + 2 * m + j] * wide, wide), wide)
                tokens[:, here] = toks[m][j * depth : (j + 1) * depth, :]

    for ref, k, skip in zip(ds, (0, 1, 3, 2, 2), (0, 0, 0, 0, 1)):
        d = ref[...].astype(F32)
        rows = d.shape[0]
        here = pl.ds(pl.multiple_of(spots[k] * ds[0].shape[0] + skip * rows, rows), rows)
        both[here, :NARROW] = (d * slope[here, :]).astype(BF)
        both[here, NARROW:] = (d * active[here, :]).astype(BF)
    weights[:, :NARROW] = w_gate[...]
    weights[:, NARROW:] = w_up[...]
    both_d = both[...]
    total[...] += times_transposed(both_d, weights[...])
    grads = (jnp.dot(tokens[...], both_d, preferred_element_type=F32) * factor).astype(BF)
    grad_gate[...] = grads[:, :NARROW]
    grad_up[...] = grads[:, NARROW:]

    @pl.when(c == pl.num_programs(0) - 1)
    def _():
        back[...] = total[...].astype(back.dtype)


def back_of(spots, half, ds, slope, active, w_gate, w_up, toks, factor, before):
    rows, part = ds[0].shape
    depth, width = w_gate.shape
    total = 4 * rows
    steps = part // NARROW
    pieces = [pl.BlockSpec((d.shape[0], NARROW), lambda c, w: (0, c)) for d in ds]
    weight = pl.BlockSpec((depth, NARROW), lambda c, w: (0, c + half * steps))
    full = pl.BlockSpec((total, NARROW), lambda c, w: (0, c + half * steps))
    whole = pl.BlockSpec((total, depth), lambda c, w: (0, 0))
    kept = [whole] + [pl.BlockSpec(memory_space=pl.ANY)] * 2 if before else []
    return pl.pallas_call(
        functools.partial(back_kernel, factor, not before),
        out_shape=(
            jax.ShapeDtypeStruct((depth, width), BF),
            jax.ShapeDtypeStruct((depth, width), BF),
            jax.ShapeDtypeStruct((total, depth), BF if before else F32),
        ),
        grid_spec=pltpu.PrefetchScalarGridSpec(
            num_scalar_prefetch=1,
            grid=(steps,),
            in_specs=pieces
            + [full, full, weight, weight]
            + [pl.BlockSpec(t.shape, lambda c, w: (0, 0)) for t in toks]
            + kept,
            out_specs=(weight, weight, whole),
            scratch_shapes=[
                pltpu.VMEM((total, 2 * NARROW), BF),
                pltpu.VMEM((depth, 2 * NARROW), BF),
                pltpu.VMEM((total, depth), F32),
                pltpu.VMEM((depth, total), BF),
            ],
        ),
        input_output_aliases={15: 0, 16: 1} if before else {},
        cost_estimate=pl.CostEstimate(
            flops=8 * total * part * depth, bytes_accessed=total * part * 14, transcendentals=0
        ),
    )(spots, *ds, slope, active, w_gate, w_up, *toks, *before)


def local(tokens, grad_out, gate_pre, up_pre, w_gate, w_up, w_down):
    rows, width = tokens.shape
    factor = float(1.0 / np.sqrt(np.float32(16 * rows)))
    y, zh = lax.axis_index("y"), lax.axis_index("zh")
    x, zl = lax.axis_index("x"), lax.axis_index("zl")
    p = lax.iota(jnp.int32, 14)
    spots = jnp.where(p < 4, lax.rem(y + p, 4), jnp.where(p == 4, zh, 1 - zh))
    m = p - 6
    far = jnp.where(lax.rem(m, 2) == 0, zl, 1 - zl) * 4 + lax.rem(x + m // 2, 4)
    spots = jnp.where(p < 6, spots, far)

    out_all = gather_col(grad_out)

    both = jnp.concatenate([gate_pre, up_pre], axis=0)
    both3, both1 = along_y(both, 1), along_y(both, -1)
    low3 = both3[:rows]
    high1 = both1[rows:]
    g2, u2 = along_y(low3, 1), along_y(high1, -1)
    paired = {k: (v, to_pair(v)) for k, v in ((0, both), (3, both3), (1, both1))}
    saved = {k: (v, v) for k, v in paired.items()}
    saved[2] = ((g2, to_pair(g2)), (u2, to_pair(u2)))

    part_rows = w_down.shape[0] // 2

    def gathered(h):
        part = times_transposed(out_all, w_down[h * part_rows : (h + 1) * part_rows]).astype(BF)
        recv = lax.all_to_all(part.reshape(4, 2 * rows, part_rows), "y", 0, 0, tiled=True)
        total = jnp.sum(recv.astype(F32), axis=0)
        mine = total.astype(BF)
        d = (total + to_pair(mine).astype(F32)).astype(BF)
        d3, d1 = along_y(d, 1), along_y(d, -1)
        return [d, d1, d3, along_y(d3[:rows], 1), along_y(d1[rows:], -1)]

    halves = [gathered(h) for h in (0, 1)]

    turned = tokens.T
    near = lax.ppermute(turned, "zl", SWAP)
    pair = jnp.concatenate([turned, near], axis=0)
    toks = [pair]
    for m in (1, 2, 3):
        toks.append(lax.ppermute(pair, "x", ring(-m)))

    def both_cores(own):
        other = lax.ppermute(own, "core", SWAP)
        return (own.astype(F32) + other.astype(F32)).astype(BF)

    kept = ()
    for k in (0, 3, 1, 2):
        kept = hidden_of(spots, k, rows, *saved[k], kept)
    hidden, slope, active = kept
    down = (inner_rows(hidden, out_all) * factor).astype(BF)
    grad_down = both_cores(down)
    before = ()
    for h in (0, 1):
        gate, up, back = back_of(spots, h, halves[h], slope, active, w_gate, w_up, toks, factor, before)
        before = (back, gate, up)
    back_recv = across_col(back.reshape(8, rows, width))
    grad_gate = both_cores(gate)
    grad_up = both_cores(up)
    grad_tokens = jnp.sum(back_recv.astype(F32), axis=0).astype(BF)
    return grad_tokens, grad_gate, grad_up, grad_down


def solution(mesh):
    fine = Mesh(mesh.devices.reshape(4, 2, 2, 4, 2), ("y", "zh", "zl", "x", "core"))
    row, col = ("y", "zh"), COL
    act = P(col + ("core",), row)
    pre = P(row + ("core",), col)
    up = P(row, col)
    down = P(col, row)

    return jax.shard_map(
        local,
        mesh=fine,
        in_specs=(act, act, pre, pre, up, up, down),
        out_specs=(act, up, up, down),
        check_vma=False,
    )
```

```python
import functools

import jax
import jax.numpy as jnp
import numpy as np
from jax import lax
from jax.experimental import pallas as pl
from jax.experimental.pallas import tpu as pltpu
from jax.sharding import Mesh, PartitionSpec as P


COL = ("zl", "x")
BF = jnp.bfloat16
F32 = jnp.float32
SWAP = [(0, 1), (1, 0)]
STEP = 512
NARROW = 256


def ring(shift):
    return [(i, (i + shift) % 4) for i in range(4)]


def along_y(x, shift):
    return lax.ppermute(x, "y", ring(shift))


def to_pair(x):
    return lax.ppermute(x, "zh", SWAP)


def across_col(x):
    return lax.all_to_all(x, COL, 0, 0, tiled=True)


def gather_col(x):
    many = jnp.broadcast_to(x[None], (8,) + x.shape)
    whole = across_col(many)
    return whole.reshape(8 * x.shape[0], x.shape[1])


def inner_rows(left, right):
    return lax.dot_general(left, right, (((0,), (0,)), ((), ())), preferred_element_type=F32)


def times_transposed(left, right):
    return lax.dot_general(left, right, (((1,), (1,)), ((), ())), preferred_element_type=F32)


def place(where, p, rows):
    return pl.ds(pl.multiple_of(where[p] * rows, rows), rows)


def hidden_kernel(spots, *refs):
    gates, ups = refs[:2], refs[2:4]
    hidden, slope, active = refs[-3:]
    rows = gates[0].shape[0]
    for j in range(2):
        g = gates[j][...].astype(F32)
        u = ups[j][...].astype(F32)
        s = 0.5 * jnp.tanh(0.5 * g) + 0.5
        here = place(spots, 4 + j, rows)
        act = g * s
        hidden[here, :] = (act * u).astype(BF)
        slope[here, :] = u * s * (1.0 + g * (1.0 - s))
        active[here, :] = act


def piece_of(rows, which):
    return pl.BlockSpec((rows, STEP), lambda c, w: (which, c))


def hidden_of(spots, k, rows, gates, ups, before):
    width = gates[0].shape[1]
    total = 8 * rows
    pieces = [piece_of(rows, 0)] * 2 + [piece_of(rows, u.shape[0] // rows - 1) for u in ups]
    pair = pl.BlockSpec((2 * rows, STEP), lambda c, w: (w[k], c))
    kept = [pl.BlockSpec(memory_space=pl.ANY)] * len(before)
    return pl.pallas_call(
        hidden_kernel,
        out_shape=(
            jax.ShapeDtypeStruct((total, width), BF),
            jax.ShapeDtypeStruct((total, width), F32),
            jax.ShapeDtypeStruct((total, width), F32),
        ),
        grid_spec=pltpu.PrefetchScalarGridSpec(
            num_scalar_prefetch=1,
            grid=(width // STEP,),
            in_specs=pieces + kept,
            out_specs=(pair, pair, pair),
        ),
        input_output_aliases={5 + i: i for i in range(len(before))},
        cost_estimate=pl.CostEstimate(
            flops=2 * rows * width * 10, bytes_accessed=2 * rows * width * 14, transcendentals=2 * rows * width * 2
        ),
    )(spots, *gates, *ups, *before)


def back_kernel(factor, far, *refs):
    ds, refs = refs[:10], refs[10:]
    slope, active, w_gate, w_up = refs[:4]
    toks, refs = refs[4:8], refs[8:]
    grad_gate, grad_up, back, both, weights, total, tokens = refs
    c = pl.program_id(0)
    half = pl.num_programs(0) // 2

    @pl.when(c == 0)
    def _():
        total[...] = jnp.zeros_like(total)
        depth, wide = tokens.shape[0], toks[0].shape[1]
        for m in range(4):
            for j in range(2):
                here = pl.ds(pl.multiple_of(far[2 * m + j] * wide, wide), wide)
                tokens[:, here] = toks[m][j * depth : (j + 1) * depth, :]

    def scaled(parts):
        for ref, k, skip in zip(parts, (0, 1, 3, 2, 2), (0, 0, 0, 0, 1)):
            d = ref[...].astype(F32)
            rows = d.shape[0]
            here = pl.ds(pl.multiple_of(far[8 + k] * parts[0].shape[0] + skip * rows, rows), rows)
            both[here, :NARROW] = (d * slope[here, :]).astype(BF)
            both[here, NARROW:] = (d * active[here, :]).astype(BF)

    @pl.when(c < half)
    def _():
        scaled(ds[:5])

    @pl.when(c >= half)
    def _():
        scaled(ds[5:])

    weights[:, :NARROW] = w_gate[...]
    weights[:, NARROW:] = w_up[...]
    both_d = both[...]
    total[...] += times_transposed(both_d, weights[...])
    grads = (jnp.dot(tokens[...], both_d, preferred_element_type=F32) * factor).astype(BF)
    grad_gate[...] = grads[:, :NARROW]
    grad_up[...] = grads[:, NARROW:]

    @pl.when(c == pl.num_programs(0) - 1)
    def _():
        back[...] = total[...].astype(back.dtype)


def back_of(far, halves, slope, active, w_gate, w_up, toks, factor):
    depth, width = w_gate.shape
    total = slope.shape[0]
    steps = width // NARROW
    half = steps // 2
    early = [pl.BlockSpec((d.shape[0], NARROW), lambda c, w: (0, jnp.minimum(c, half - 1))) for d in halves[0]]
    late = [pl.BlockSpec((d.shape[0], NARROW), lambda c, w: (0, jnp.maximum(c - half, 0))) for d in halves[1]]
    weight = pl.BlockSpec((depth, NARROW), lambda c, w: (0, c))
    full = pl.BlockSpec((total, NARROW), lambda c, w: (0, c))
    whole = pl.BlockSpec((total, depth), lambda c, w: (0, 0))
    return pl.pallas_call(
        functools.partial(back_kernel, factor),
        out_shape=(
            jax.ShapeDtypeStruct((depth, width), BF),
            jax.ShapeDtypeStruct((depth, width), BF),
            jax.ShapeDtypeStruct((total, depth), BF),
        ),
        grid_spec=pltpu.PrefetchScalarGridSpec(
            num_scalar_prefetch=1,
            grid=(steps,),
            in_specs=early
            + late
            + [full, full, weight, weight]
            + [pl.BlockSpec(t.shape, lambda c, w: (0, 0)) for t in toks],
            out_specs=(weight, weight, whole),
            scratch_shapes=[
                pltpu.VMEM((total, 2 * NARROW), BF),
                pltpu.VMEM((depth, 2 * NARROW), BF),
                pltpu.VMEM((total, depth), F32),
                pltpu.VMEM((depth, total), BF),
            ],
        ),
        cost_estimate=pl.CostEstimate(
            flops=8 * total * width * depth, bytes_accessed=total * width * 14, transcendentals=0
        ),
    )(far, *halves[0], *halves[1], slope, active, w_gate, w_up, *toks)


def local(tokens, grad_out, gate_pre, up_pre, w_gate, w_up, w_down):
    rows, width = tokens.shape
    factor = float(1.0 / np.sqrt(np.float32(16 * rows)))
    y, zh = lax.axis_index("y"), lax.axis_index("zh")
    x, zl = lax.axis_index("x"), lax.axis_index("zl")
    p = lax.iota(jnp.int32, 6)
    spots = jnp.where(p < 4, lax.rem(y + p, 4), jnp.where(p == 4, zh, 1 - zh))
    m = lax.iota(jnp.int32, 12)
    far = jnp.where(lax.rem(m, 2) == 0, zl, 1 - zl) * 4 + lax.rem(x + m // 2, 4)
    far = jnp.where(m < 8, far, lax.rem(y + m, 4))

    out_all = gather_col(grad_out)

    both = jnp.concatenate([gate_pre, up_pre], axis=0)
    both3, both1 = along_y(both, 1), along_y(both, -1)
    low3 = both3[:rows]
    high1 = both1[rows:]
    g2, u2 = along_y(low3, 1), along_y(high1, -1)
    paired = {k: (v, to_pair(v)) for k, v in ((0, both), (3, both3), (1, both1))}
    saved = {k: (v, v) for k, v in paired.items()}
    saved[2] = ((g2, to_pair(g2)), (u2, to_pair(u2)))

    part_rows = w_down.shape[0] // 2

    def gathered(h):
        part = times_transposed(out_all, w_down[h * part_rows : (h + 1) * part_rows]).astype(BF)
        recv = lax.all_to_all(part.reshape(4, 2 * rows, part_rows), "y", 0, 0, tiled=True)
        total = jnp.sum(recv.astype(F32), axis=0)
        mine = total.astype(BF)
        d = (total + to_pair(mine).astype(F32)).astype(BF)
        d3, d1 = along_y(d, 1), along_y(d, -1)
        return [d, d1, d3, along_y(d3[:rows], 1), along_y(d1[rows:], -1)]

    halves = [gathered(h) for h in (0, 1)]

    turned = tokens.T
    near = lax.ppermute(turned, "zl", SWAP)
    pair = jnp.concatenate([turned, near], axis=0)
    toks = [pair]
    for m in (1, 2, 3):
        toks.append(lax.ppermute(pair, "x", ring(-m)))

    def both_cores(own):
        other = lax.ppermute(own, "core", SWAP)
        return (own.astype(F32) + other.astype(F32)).astype(BF)

    kept = ()
    for k in (0, 3, 1, 2):
        kept = hidden_of(spots, k, rows, *saved[k], kept)
    hidden, slope, active = kept
    down = (inner_rows(hidden, out_all) * factor).astype(BF)
    grad_down = both_cores(down)
    gate, up, back = back_of(far, halves, slope, active, w_gate, w_up, toks, factor)
    back_recv = across_col(back.reshape(8, rows, width))
    grad_gate = both_cores(gate)
    grad_up = both_cores(up)
    grad_tokens = jnp.sum(back_recv.astype(F32), axis=0).astype(BF)
    return grad_tokens, grad_gate, grad_up, grad_down


def solution(mesh):
    fine = Mesh(mesh.devices.reshape(4, 2, 2, 4, 2), ("y", "zh", "zl", "x", "core"))
    row, col = ("y", "zh"), COL
    act = P(col + ("core",), row)
    pre = P(row + ("core",), col)
    up = P(row, col)
    down = P(col, row)

    return jax.shard_map(
        local,
        mesh=fine,
        in_specs=(act, act, pre, pre, up, up, down),
        out_specs=(act, up, up, down),
        check_vma=False,
    )
```

```python
import functools

import jax
import jax.numpy as jnp
import numpy as np
from jax import lax
from jax.experimental import pallas as pl
from jax.experimental.pallas import tpu as pltpu
from jax.sharding import Mesh, PartitionSpec as P


COL = ("zl", "x")
BF = jnp.bfloat16
F32 = jnp.float32
SWAP = [(0, 1), (1, 0)]
STEP = 512
NARROW = 512


def ring(shift):
    return [(i, (i + shift) % 4) for i in range(4)]


def along_y(x, shift):
    return lax.ppermute(x, "y", ring(shift))


def to_pair(x):
    return lax.ppermute(x, "zh", SWAP)


def across_col(x):
    return lax.all_to_all(x, COL, 0, 0, tiled=True)


def gather_col(x):
    many = jnp.broadcast_to(x[None], (8,) + x.shape)
    whole = across_col(many)
    return whole.reshape(8 * x.shape[0], x.shape[1])


def inner_rows(left, right):
    return lax.dot_general(left, right, (((0,), (0,)), ((), ())), preferred_element_type=F32)


def times_transposed(left, right):
    return lax.dot_general(left, right, (((1,), (1,)), ((), ())), preferred_element_type=F32)


def place(where, p, rows):
    return pl.ds(pl.multiple_of(where[p] * rows, rows), rows)


def hidden_kernel(spots, *refs):
    gates, ups = refs[:2], refs[2:4]
    hidden, slope, active = refs[-3:]
    rows = gates[0].shape[0]
    for j in range(2):
        g = gates[j][...].astype(F32)
        u = ups[j][...].astype(F32)
        s = 0.5 * jnp.tanh(0.5 * g) + 0.5
        here = place(spots, 4 + j, rows)
        act = g * s
        hidden[here, :] = (act * u).astype(BF)
        slope[here, :] = u * s * (1.0 + g * (1.0 - s))
        active[here, :] = act


def piece_of(rows, which):
    return pl.BlockSpec((rows, STEP), lambda c, w: (which, c))


def hidden_of(spots, k, rows, gates, ups, before):
    width = gates[0].shape[1]
    total = 8 * rows
    pieces = [piece_of(rows, 0)] * 2 + [piece_of(rows, u.shape[0] // rows - 1) for u in ups]
    pair = pl.BlockSpec((2 * rows, STEP), lambda c, w: (w[k], c))
    kept = [pl.BlockSpec(memory_space=pl.ANY)] * len(before)
    return pl.pallas_call(
        hidden_kernel,
        out_shape=(
            jax.ShapeDtypeStruct((total, width), BF),
            jax.ShapeDtypeStruct((total, width), F32),
            jax.ShapeDtypeStruct((total, width), F32),
        ),
        grid_spec=pltpu.PrefetchScalarGridSpec(
            num_scalar_prefetch=1,
            grid=(width // STEP,),
            in_specs=pieces + kept,
            out_specs=(pair, pair, pair),
        ),
        input_output_aliases={5 + i: i for i in range(len(before))},
        cost_estimate=pl.CostEstimate(
            flops=2 * rows * width * 10, bytes_accessed=2 * rows * width * 14, transcendentals=2 * rows * width * 2
        ),
    )(spots, *gates, *ups, *before)


def back_kernel(factor, far, *refs):
    ds, refs = refs[:10], refs[10:]
    slope, active, w_gate, w_up = refs[:4]
    toks, refs = refs[4:8], refs[8:]
    grad_gate, grad_up, back, both, weights, total, tokens = refs
    c = pl.program_id(0)
    half = pl.num_programs(0) // 2

    @pl.when(c == 0)
    def _():
        total[...] = jnp.zeros_like(total)
        depth, wide = tokens.shape[0], toks[0].shape[1]
        for m in range(4):
            for j in range(2):
                here = pl.ds(pl.multiple_of(far[2 * m + j] * wide, wide), wide)
                tokens[:, here] = toks[m][j * depth : (j + 1) * depth, :]

    def scaled(parts):
        for ref, k, skip in zip(parts, (0, 1, 3, 2, 2), (0, 0, 0, 0, 1)):
            d = ref[...].astype(F32)
            rows = d.shape[0]
            here = pl.ds(pl.multiple_of(far[8 + k] * parts[0].shape[0] + skip * rows, rows), rows)
            both[here, :NARROW] = (d * slope[here, :]).astype(BF)
            both[here, NARROW:] = (d * active[here, :]).astype(BF)

    @pl.when(c < half)
    def _():
        scaled(ds[:5])

    @pl.when(c >= half)
    def _():
        scaled(ds[5:])

    weights[:, :NARROW] = w_gate[...]
    weights[:, NARROW:] = w_up[...]
    both_d = both[...]
    total[...] += times_transposed(both_d, weights[...])
    grads = (jnp.dot(tokens[...], both_d, preferred_element_type=F32) * factor).astype(BF)
    grad_gate[...] = grads[:, :NARROW]
    grad_up[...] = grads[:, NARROW:]

    @pl.when(c == pl.num_programs(0) - 1)
    def _():
        back[...] = total[...].astype(back.dtype)


def back_of(far, halves, slope, active, w_gate, w_up, toks, factor):
    depth, width = w_gate.shape
    total = slope.shape[0]
    steps = width // NARROW
    half = steps // 2
    early = [pl.BlockSpec((d.shape[0], NARROW), lambda c, w: (0, jnp.minimum(c, half - 1))) for d in halves[0]]
    late = [pl.BlockSpec((d.shape[0], NARROW), lambda c, w: (0, jnp.maximum(c - half, 0))) for d in halves[1]]
    weight = pl.BlockSpec((depth, NARROW), lambda c, w: (0, c))
    full = pl.BlockSpec((total, NARROW), lambda c, w: (0, c))
    whole = pl.BlockSpec((total, depth), lambda c, w: (0, 0))
    return pl.pallas_call(
        functools.partial(back_kernel, factor),
        out_shape=(
            jax.ShapeDtypeStruct((depth, width), BF),
            jax.ShapeDtypeStruct((depth, width), BF),
            jax.ShapeDtypeStruct((total, depth), BF),
        ),
        grid_spec=pltpu.PrefetchScalarGridSpec(
            num_scalar_prefetch=1,
            grid=(steps,),
            in_specs=early
            + late
            + [full, full, weight, weight]
            + [pl.BlockSpec(t.shape, lambda c, w: (0, 0)) for t in toks],
            out_specs=(weight, weight, whole),
            scratch_shapes=[
                pltpu.VMEM((total, 2 * NARROW), BF),
                pltpu.VMEM((depth, 2 * NARROW), BF),
                pltpu.VMEM((total, depth), F32),
                pltpu.VMEM((depth, total), BF),
            ],
        ),
        cost_estimate=pl.CostEstimate(
            flops=8 * total * width * depth, bytes_accessed=total * width * 14, transcendentals=0
        ),
    )(far, *halves[0], *halves[1], slope, active, w_gate, w_up, *toks)


def local(tokens, grad_out, gate_pre, up_pre, w_gate, w_up, w_down):
    rows, width = tokens.shape
    factor = float(1.0 / np.sqrt(np.float32(16 * rows)))
    y, zh = lax.axis_index("y"), lax.axis_index("zh")
    x, zl = lax.axis_index("x"), lax.axis_index("zl")
    p = lax.iota(jnp.int32, 6)
    spots = jnp.where(p < 4, lax.rem(y + p, 4), jnp.where(p == 4, zh, 1 - zh))
    m = lax.iota(jnp.int32, 12)
    far = jnp.where(lax.rem(m, 2) == 0, zl, 1 - zl) * 4 + lax.rem(x + m // 2, 4)
    far = jnp.where(m < 8, far, lax.rem(y + m, 4))

    out_all = gather_col(grad_out)

    both = jnp.concatenate([gate_pre, up_pre], axis=0)
    both3, both1 = along_y(both, 1), along_y(both, -1)
    low3 = both3[:rows]
    high1 = both1[rows:]
    g2, u2 = along_y(low3, 1), along_y(high1, -1)
    paired = {k: (v, to_pair(v)) for k, v in ((0, both), (3, both3), (1, both1))}
    saved = {k: (v, v) for k, v in paired.items()}
    low3p = paired[3][1][:rows]
    saved[2] = ((g2, along_y(low3p, 1)), (u2, to_pair(u2)))

    part_rows = w_down.shape[0] // 2

    def gathered(h):
        part = times_transposed(out_all, w_down[h * part_rows : (h + 1) * part_rows]).astype(BF)
        recv = lax.all_to_all(part.reshape(4, 2 * rows, part_rows), "y", 0, 0, tiled=True)
        total = jnp.sum(recv.astype(F32), axis=0)
        mine = total.astype(BF)
        d = (total + to_pair(mine).astype(F32)).astype(BF)
        d3, d1 = along_y(d, 1), along_y(d, -1)
        return [d, d1, d3, along_y(d3[:rows], 1), along_y(d1[rows:], -1)]

    halves = [gathered(h) for h in (0, 1)]

    turned = tokens.T
    near = lax.ppermute(turned, "zl", SWAP)
    pair = jnp.concatenate([turned, near], axis=0)
    toks = [pair]
    for m in (1, 2, 3):
        toks.append(lax.ppermute(pair, "x", ring(-m)))

    def both_cores(own):
        other = lax.ppermute(own, "core", SWAP)
        return (own.astype(F32) + other.astype(F32)).astype(BF)

    kept = ()
    for k in (0, 3, 1, 2):
        kept = hidden_of(spots, k, rows, *saved[k], kept)
    hidden, slope, active = kept
    down = (inner_rows(hidden, out_all) * factor).astype(BF)
    grad_down = both_cores(down)
    gate, up, back = back_of(far, halves, slope, active, w_gate, w_up, toks, factor)
    back_recv = across_col(back.reshape(8, rows, width))
    grad_gate = both_cores(gate)
    grad_up = both_cores(up)
    grad_tokens = jnp.sum(back_recv.astype(F32), axis=0).astype(BF)
    return grad_tokens, grad_gate, grad_up, grad_down


def solution(mesh):
    fine = Mesh(mesh.devices.reshape(4, 2, 2, 4, 2), ("y", "zh", "zl", "x", "core"))
    row, col = ("y", "zh"), COL
    act = P(col + ("core",), row)
    pre = P(row + ("core",), col)
    up = P(row, col)
    down = P(col, row)

    return jax.shard_map(
        local,
        mesh=fine,
        in_specs=(act, act, pre, pre, up, up, down),
        out_specs=(act, up, up, down),
        check_vma=False,
    )
```
